32 devices in a mesh: groups: 2 (over x), seq: 16 (over z, y, core).
Axes of the slice: x: 2, y: 2, z: 4, core: 2. Of those that a mesh axis runs over, the one named last changes fastest.
Arguments:
- queries: bfloat16 [8192, 2048], P(('groups', 'seq')), parts along dimension 0, may hold values from -14 to 14
- ctx_keys: bfloat16 [8192, 512], P(('groups', 'seq')), parts along dimension 0, may hold values from -11.5 to 11.5
- ctx_values: bfloat16 [8192, 512], P(('groups', 'seq')), parts along dimension 0, may hold values from -5 to 5
- store_keys: bfloat16 [512, 128, 512], P(('groups', 'seq')), parts along dimension 0, may hold values from -11.5 to 11.5
- store_values: bfloat16 [512, 128, 512], P(('groups', 'seq')), parts along dimension 0, may hold values from -5 to 5
- block_ids: int32 [32, 32], P(('groups', 'seq')), parts along dimension 0, may hold values from 0 to 255, as said below
- block_slot: int32 [512], P('groups'), parts along dimension 0, may hold values from 0 to 255, as said below
- gate_logit: float32 [16], replicated, may hold values from -2 to 2
Outputs:
- mixed: bfloat16 [8192, 2048], P(('groups', 'seq')), parts along dimension 0
The draws below stay inside these ranges and needn't reach their ends.
There are 2 independent parts, one for each index of `groups`. The reference program is written for one: setup_inputs(seed, part) draws one part's arguments, and reference() takes and returns one part's arrays. A program takes and returns all parts, laid end to end along the dimension named above; an argument that names none is the same for every part. Nothing has to cross between parts.
Inputs may be any that keep to these rules, and one draw needn't show every extreme that they name: block_slot is a permutation of 0 to 255; memory block b lies on seq index block_slot[b] // 16 at local position block_slot[b] % 16. `block_ids`: the 32 ids of one row are distinct; at most 2 of them lie on any one seq index, and in every draw some seq index holds exactly 2 blocks of every row.
All inputs are finite; a program needn't handle non-finite values.
Results may differ from the reference program's by a relative error of at most 0.0052.
Values may be sent and summed in bfloat16 or wider, within the bound.
A program may use at most 192 MiB of HBM per device.

```python
import jax
import jax.numpy as jnp
from jax import lax

H = 16
KVH = 4
HD = 128
QBLK = 256
MROWS = 128
TOPM = 32
CAP = 2
MEM_DEV = 16
TOKENS = 4096
NQB = 16
MEM_BLOCKS = 256


def route_tables(key):
    base = jax.random.fold_in(key, 4242)
    key_perm = jax.random.fold_in(base, 1)
    key_hot = jax.random.fold_in(base, 2)
    key_popular = jax.random.fold_in(base, 3)
    key_score = jax.random.fold_in(base, 4)
    key_first = jax.random.fold_in(base, 5)
    key_stride = jax.random.fold_in(base, 6)
    owners_count = MEM_BLOCKS // MEM_DEV
    slot_of = jax.random.permutation(key_perm, MEM_BLOCKS).astype(jnp.int32)
    id_of_slot = jnp.argsort(slot_of).astype(jnp.int32)
    hottest = jax.random.randint(key_hot, (), 0, owners_count)
    popular = jax.random.randint(key_popular, (owners_count,), 0, 2 ** 19)
    candidates = jnp.arange(owners_count * CAP, dtype=jnp.int32)
    cand_owner = candidates // CAP
    score = jax.random.randint(key_score, (NQB, owners_count * CAP), 0, 2 ** 19) + popular[cand_owner][None, :]
    score = score + jnp.where(cand_owner == hottest, 2 ** 21, 0)[None, :]
    score = score * (owners_count * CAP) + candidates[None, :]
    ignored, chosen = lax.top_k(score, TOPM)
    owner = chosen // CAP
    copy_no = chosen % CAP
    first = jax.random.randint(key_first, (NQB, owners_count), 0, MEM_DEV)
    stride = jax.random.randint(key_stride, (NQB, owners_count), 1, MEM_DEV)
    local = (jnp.take_along_axis(first, owner, axis=1) + copy_no * jnp.take_along_axis(stride, owner, axis=1)) % MEM_DEV
    slots = owner * MEM_DEV + local
    return (slot_of, id_of_slot[slots].astype(jnp.int32))


def draw_block_ids(key, part):
    return route_tables(key)[1]


def draw_block_slot(key, part):
    return route_tables(key)[0]


def draw_queries(key, part):
    inner = jax.random.fold_in(key, 11)
    field = jnp.clip(2.5 * jax.random.normal(inner, (TOKENS, H * HD), jnp.float32), -14.0, 14.0)
    return field.astype(jnp.bfloat16)


def draw_ctx_keys(key, part):
    inner = jax.random.fold_in(key, 12)
    field = jnp.clip(jax.random.normal(inner, (TOKENS, KVH * HD), jnp.float32), -4.0, 4.0)
    return field.astype(jnp.bfloat16)


def draw_store_keys(key, part):
    inner = jax.random.fold_in(key, 13)
    field = jnp.clip(jax.random.normal(inner, (MEM_BLOCKS, MROWS, KVH * HD), jnp.float32), -4.0, 4.0)
    return field.astype(jnp.bfloat16)


def block_scale(stream_key, shape, pieces, smallest, high):
    loudness, own = 1.0, jax.random.fold_in(stream_key, 6)
    for position, shards_of in pieces:
        draws = jnp.exp(jax.random.uniform(jax.random.fold_in(own, position), (shards_of,), jnp.float32, smallest / len(pieces), high / len(pieces)))
        loudness = loudness * jnp.repeat(draws, shape[position] // shards_of).reshape([-1 if axis == position else 1 for axis in range(len(shape))])
    return loudness


def normal_values(stream_key, shape, scale, limit, pieces=(), held_as=jnp.bfloat16):
    factor_of = block_scale(stream_key, shape, pieces, -0.22, 0.18) if pieces else 1.0
    array = jax.random.normal(stream_key, shape, jnp.float32) * scale * factor_of
    return jnp.minimum(jnp.maximum(array, -limit), limit).astype(held_as)


def setup_inputs(seed: int = 0, part: int = 0) -> dict:
    splits = jax.random.split(jax.random.key(seed), 9)
    part_keys = jax.random.split(jax.random.fold_in(splits[8], part), 9)
    queries = draw_queries(jax.random.fold_in(jax.random.fold_in(splits[8], part), 71), part)
    ctx_keys = draw_ctx_keys(jax.random.fold_in(jax.random.fold_in(splits[8], part), 71), part)
    ctx_values = normal_values(part_keys[2], (TOKENS, KVH * HD), 1.0, 5.0, ((0, 16),))
    store_keys = draw_store_keys(jax.random.fold_in(jax.random.fold_in(splits[8], part), 71), part)
    store_values = normal_values(part_keys[4], (MEM_BLOCKS, MROWS, KVH * HD), 1.0, 5.0, ((0, 16),))
    block_ids = draw_block_ids(jax.random.fold_in(jax.random.fold_in(splits[8], part), 71), part)
    block_slot = draw_block_slot(jax.random.fold_in(jax.random.fold_in(splits[8], part), 71), part)
    gate_logit = jnp.clip(jax.random.uniform(splits[7], (H,), jnp.float32, -2.0, 2.0), -2.0, 2.0)
    return {"queries": queries, "ctx_keys": ctx_keys, "ctx_values": ctx_values, "store_keys": store_keys, "store_values": store_values, "block_ids": block_ids, "block_slot": block_slot, "gate_logit": gate_logit}


def attend(query_rows, key_rows, value_rows, allowed):
    row_count = query_rows.shape[0]
    query_heads = query_rows.astype(jnp.float32).reshape(row_count, KVH, H // KVH, HD)
    key_heads = key_rows.astype(jnp.float32).reshape(-1, KVH, HD)
    value_heads = value_rows.astype(jnp.float32).reshape(-1, KVH, HD)
    scores = jnp.einsum("rhgd,khd->hgrk", query_heads, key_heads) * (HD ** -0.5)
    if allowed is not None:
        scores = jnp.where(allowed[None, None], scores, -1e30)
    row_max = jnp.max(scores, axis=-1, keepdims=True)
    probs = jnp.exp(scores - row_max)
    total = jnp.sum(probs, axis=-1)
    rounded = lax.optimization_barrier(probs.astype(jnp.bfloat16)).astype(jnp.float32)
    weighted = jnp.einsum("hgrk,khd->hgrd", rounded, value_heads)
    result = weighted / total[..., None]
    return jnp.transpose(result, (2, 0, 1, 3)).reshape(row_count, H * HD).astype(jnp.bfloat16)


def reference(queries, ctx_keys, ctx_values, store_keys, store_values, block_ids, block_slot, gate_logit):
    positions = jnp.arange(TOKENS, dtype=jnp.int32)
    gate = jnp.repeat(jax.nn.sigmoid(gate_logit.astype(jnp.float32)), HD)

    def one_block(block_no):
        start = (block_no * QBLK).astype(jnp.int32)
        query_rows = lax.dynamic_slice_in_dim(queries, start, QBLK, 0)
        query_pos = start + jnp.arange(QBLK, dtype=jnp.int32)
        allowed = positions[None, :] <= query_pos[:, None]
        context = attend(query_rows, ctx_keys, ctx_values, allowed)
        slots = block_slot[block_ids[block_no]]
        memory_keys = store_keys[slots].reshape(TOPM * MROWS, KVH * HD)
        memory_values = store_values[slots].reshape(TOPM * MROWS, KVH * HD)
        memory = attend(query_rows, memory_keys, memory_values, None)
        memory_wide = lax.optimization_barrier(memory).astype(jnp.float32)
        context_wide = lax.optimization_barrier(context).astype(jnp.float32)
        return (gate * memory_wide + (1.0 - gate) * context_wide).astype(jnp.bfloat16)

    blocks = lax.map(one_block, jnp.arange(NQB, dtype=jnp.int32))
    return blocks.reshape(TOKENS, H * HD)
```

```python
import functools

import jax
import jax.numpy as jnp
from jax import lax
from jax.experimental import pallas as pl
from jax.experimental.pallas import tpu as pltpu
from jax.sharding import PartitionSpec as P

H = 16
KVH = 4
HD = 128
GROUP = H // KVH
QBLK = 256
MROWS = 128
TOPM = 32
CAP = 2
CELL = 2 * KVH
PAIR = 2
WIDTH = PAIR * HD
TILE = 1024
SPAN = CELL * QBLK // TILE
PICKS = CELL * CAP
PER_TILE = TILE // MROWS

NEG = -1e30
SCALE2 = HD ** (-0.5) * 1.4426950408889634
VMEM_LIMIT = 60 * 1024 * 1024
MESH = pl.DeviceIdType.MESH


def request_table(slots, owners_count, capacity, local_count):
    entries = slots.shape[0]
    owner = slots // local_count
    local = slots % local_count
    order = jnp.arange(entries, dtype=jnp.int32)
    earlier = (owner[:, None] == owner[None, :]) & (order[None, :] < order[:, None])
    rank = jnp.sum(earlier.astype(jnp.int32), axis=1)
    chosen = (owner[:, None, None] == jnp.arange(owners_count, dtype=jnp.int32)[None, :, None]) & (
        rank[:, None, None] == jnp.arange(capacity, dtype=jnp.int32)[None, None, :]
    )
    return jnp.sum(jnp.where(chosen, local[:, None, None] + 1, 0), axis=0) - 1


def lookup_slots(wanted_ids, block_slot):
    hits = wanted_ids[..., None] == jnp.arange(block_slot.shape[0], dtype=jnp.int32)
    return jnp.sum(jnp.where(hits, block_slot, 0), axis=-1)


def fresh(rows):
    return (
        jnp.full((rows, 1), NEG, jnp.float32),
        jnp.zeros((rows, 1), jnp.float32),
        jnp.zeros((rows, HD), jnp.float32),
    )


def scores(q, k):
    return lax.dot_general(q, k, (((1,), (1,)), ((), ())), preferred_element_type=jnp.float32)


def absorb(state, s, v):
    if state is None:
        m = jnp.max(s, axis=-1, keepdims=True)
        p = jnp.exp2((s - m) * SCALE2)
        l = jnp.sum(p, axis=-1, keepdims=True)
        return m, l, jnp.dot(p.astype(jnp.bfloat16), v, preferred_element_type=jnp.float32)
    m, l, acc = state
    m_new = jnp.maximum(m, jnp.max(s, axis=-1, keepdims=True))
    decay = jnp.exp2((m - m_new) * SCALE2)
    p = jnp.exp2((s - m_new) * SCALE2)
    l = l * decay + jnp.sum(p, axis=-1, keepdims=True)
    acc = acc * decay + jnp.dot(p.astype(jnp.bfloat16), v, preferred_element_type=jnp.float32)
    return m_new, l, acc


def run_steps(states, steps):
    states = list(states)
    ahead = scores(*steps[0][1:3])
    for n, (head, _, _, v, change) in enumerate(steps):
        s = ahead
        if n + 1 < len(steps):
            ahead = scores(*steps[n + 1][1:3])
        if change is not None:
            s = change(s)
        states[head] = absorb(states[head], s, v)
    return tuple(states)


def attention_kernel(size, masked, gate_ref, table_ref, q_ref, key_ref, value_ref, sk_ref, sv_ref, out_ref,
                     tb, qs, ck, cv, sk, sv, ctx, po, ro, ps, rs, os,
                     t_sem, q_sem, kv_send, kv_recv, kv_fwd, st_send, st_recv, st_fwd,
                     po_sem, ps_sem, out_sem, self_sem):
    cells = size // CELL
    chips = size // 2
    me = lax.axis_index("seq")
    cell = me // CELL
    spot = me % CELL
    chip = me // 2
    head = chip % KVH
    core = me % 2
    peer = chip * 2 + 1 - core
    rows = q_ref.shape[0]
    local = sk_ref.shape[0]

    def lanes_of(j, width):
        return pl.ds(pl.multiple_of(j * width, width), width)

    def remote(src, dst, send, recv, device):
        return pltpu.make_async_remote_copy(
            src_ref=src, dst_ref=dst, send_sem=send, recv_sem=recv,
            device_id={"seq": device}, device_id_type=MESH,
        )

    def table_copy(step):
        return remote(table_ref, tb.at[me], t_sem.at[0, step], t_sem.at[1, me], (me + step) % size)

    def table_arrival(step):
        return remote(table_ref, tb.at[(me + step) % size], t_sem.at[0, step], t_sem.at[1, (me + step) % size], peer)

    def query_copy(device):
        return remote(q_ref.at[:, lanes_of(device % CELL, WIDTH)], qs.at[me],
                      q_sem.at[0, device], q_sem.at[1, me], device)

    def query_arrival(device):
        return remote(qs.at[device], qs.at[device], q_sem.at[0, device], q_sem.at[1, device], peer)

    def context_copies(other):
        return tuple(
            remote(src.at[:, lanes_of(other % KVH, HD)], dst.at[me],
                   kv_send.at[w, other], kv_recv.at[w, me], other * 2 + core)
            for w, (src, dst) in enumerate(((key_ref, ck), (value_ref, cv)))
        )

    def context_forwards(source):
        return tuple(
            remote(buf.at[source], buf.at[source], kv_fwd.at[w, source // 2], kv_recv.at[w, source], peer)
            for w, buf in enumerate((ck, cv))
        )

    def owned(o):
        return pl.ds(pl.multiple_of(o * local, local), local)

    def store_copies(other):
        return tuple(
            remote(src.at[:, :, lanes_of(other, HD)], dst.at[owned(spot)],
                   st_send.at[w, other], st_recv.at[w, spot], cell * CELL + other * 2 + core)
            for w, (src, dst) in enumerate(((sk_ref, sk), (sv_ref, sv)))
        )

    def store_forwards(o):
        return tuple(
            remote(buf.at[owned(o)], buf.at[owned(o)], st_fwd.at[w, o // 2], st_recv.at[w, o], peer)
            for w, buf in enumerate((sk, sv))
        )

    def self_copies():
        return (
            pltpu.make_async_copy(table_ref, tb.at[me], self_sem.at[0]),
            pltpu.make_async_copy(q_ref.at[:, lanes_of(spot, WIDTH)], qs.at[me], self_sem.at[1]),
            pltpu.make_async_copy(key_ref.at[:, lanes_of(head, HD)], ck.at[me], self_sem.at[2]),
            pltpu.make_async_copy(value_ref.at[:, lanes_of(head, HD)], cv.at[me], self_sem.at[3]),
            pltpu.make_async_copy(sk_ref.at[:, :, lanes_of(head, HD)], sk.at[owned(spot)], self_sem.at[4]),
            pltpu.make_async_copy(sv_ref.at[:, :, lanes_of(head, HD)], sv.at[owned(spot)], self_sem.at[5]),
        )

    def partial_copy(slot):
        away = (cell + 1 + slot // CELL) % cells
        return remote(po.at[slot], ro.at[slot], po_sem.at[0, slot], po_sem.at[1, slot], away * CELL + spot)

    def stats_copy(c):
        return remote(ps.at[c], rs.at[c], ps_sem.at[0, c], ps_sem.at[1, c], (cell + 1 + c) % cells * CELL + spot)

    def result_copy(i):
        return remote(os.at[i], out_ref.at[:, lanes_of(spot, WIDTH)],
                      out_sem.at[0, i], out_sem.at[1, spot], cell * CELL + i)

    def result_arrival(u):
        return remote(os.at[0], out_ref.at[:, lanes_of(u, WIDTH)], out_sem.at[0, u], out_sem.at[1, u], peer)

    def result_self():
        return pltpu.make_async_copy(os.at[spot], out_ref.at[:, lanes_of(spot, WIDTH)], self_sem.at[6])

    def each(low, high, body):
        def step(i, carry):
            body(i)
            return carry

        lax.fori_loop(low, high, step, 0)

    def start(*copies):
        for copy in copies:
            copy.start()

    mine = self_copies()
    start(*mine)

    barrier = pltpu.get_barrier_semaphore()
    each(1, size, lambda step: pl.semaphore_signal(
        barrier, inc=1, device_id={"seq": (me + step) % size}, device_id_type=MESH))
    pl.semaphore_wait(barrier, size - 1)

    each(1, size, lambda step: table_copy(step).start())
    each(1, CELL, lambda step: query_copy(cell * CELL + (spot + step) % CELL).start())
    each(CELL, size, lambda step: query_copy((cell * CELL + step // CELL * CELL + (spot + step) % CELL) % size).start())

    def send_context(step):
        other = (chip + step) % chips

        @pl.when(other // KVH >= cell)
        def _():
            start(*context_copies(other))

    each(1, chips, send_context)
    each(1, KVH, lambda step: start(*store_copies((head + step) % KVH)))

    mine[2].wait()
    mine[3].wait()
    start(*context_forwards(me))
    mine[4].wait()
    mine[5].wait()
    start(*store_forwards(spot))

    def relay_context(step):
        other = (chip + step) % chips

        @pl.when(other // KVH <= cell)
        def _():
            for copy in context_forwards(other * 2 + core):
                copy.wait_recv()
            start(*context_forwards(other * 2 + core))

    each(1, chips, relay_context)

    def arrive_context(other):
        for copy in context_forwards(other * 2 + 1 - core):
            copy.wait_recv()

    each(0, (cell + 1) * KVH, arrive_context)

    mine[1].wait()
    each(1, CELL, lambda step: query_arrival(cell * CELL + (spot + step) % CELL).wait_recv())

    def head_of(b, n):
        return qs[b, :, n * HD:(n + 1) * HD]

    def context_tile(t):
        at = pl.ds(t * (TILE // QBLK), TILE // QBLK)
        return ck[at].reshape(TILE, HD), cv[at].reshape(TILE, HD)

    def context_query(i, late):
        b = cell * CELL + i
        q = [head_of(b, n) for n in range(PAIR)]
        spots = i % (TILE // QBLK) * rows + lax.broadcasted_iota(jnp.int32, (rows, TILE), 0)
        allowed = lax.broadcasted_iota(jnp.int32, (rows, TILE), 1) <= spots

        def causal(s):
            return jnp.where(allowed, s, NEG)

        first = cell * SPAN
        steps = []
        if late:
            k, v = context_tile(first)
            steps += [(n, q[n], k, v, None) for n in range(PAIR)]
        k, v = context_tile(first + (1 if late else 0))
        steps += [(n, q[n], k, v, causal) for n in range(PAIR)]
        states = run_steps((None, None), steps)

        def earlier(c, states):
            steps = []
            for t in range(SPAN):
                k, v = context_tile(c * SPAN + t)
                steps += [(n, q[n], k, v, None) for n in range(PAIR)]
            return run_steps(states, steps)

        states = lax.fori_loop(0, cell, earlier, states)
        for n in range(PAIR):
            m, l, acc = states[n]
            ctx[i, :, n * HD:(n + 1) * HD] = (acc / l).astype(jnp.bfloat16)

    half = TILE // QBLK
    each(0, half, lambda i: context_query(i, False))
    each(half, CELL, lambda i: context_query(i, True))

    def relay_store(step):
        o = (head + step) % KVH * 2 + core
        for copy in store_forwards(o):
            copy.wait_recv()
        start(*store_forwards(o))

    each(1, KVH, relay_store)

    def arrive_store(other):
        for copy in store_forwards(other * 2 + 1 - core):
            copy.wait_recv()

    each(0, KVH, arrive_store)
    mine[0].wait()
    each(1, size, lambda step: table_arrival(step).wait_recv())

    lane = lax.broadcasted_iota(jnp.int32, (rows, HD), 1)

    def memory_states(b):
        q = [head_of(b, n) for n in range(PAIR)]
        steps = []
        for t in range(PICKS // PER_TILE):
            ks, vs, gone = [], [], []
            for x in range(PER_TILE):
                pick = t * PER_TILE + x
                there = tb[b, cell * PICKS + pick]
                at = pick // CAP * local + jnp.maximum(there, 0)
                ks.append(sk[at])
                vs.append(sv[at])
                gone.append(jnp.where(there < 0, NEG, 0.0).astype(jnp.float32))
            k, v = jnp.concatenate(ks, axis=0), jnp.concatenate(vs, axis=0)

            def hide(s, gone=gone):
                return jnp.concatenate(
                    [s[:, x * MROWS:(x + 1) * MROWS] + gone[x] for x in range(PER_TILE)], axis=1
                )

            steps += [(n, q[n], k, v, hide if masked else None) for n in range(PAIR)]
        return run_steps((None, None), steps)

    each(CELL, size, lambda step: query_arrival(
        (cell * CELL + step // CELL * CELL + step % CELL) % size).wait_recv())

    for c in range(cells - 1):

        def serve(i, stats, c=c):
            b = (cell + 1 + c) % cells * CELL + i
            states = memory_states(b)
            for n in range(PAIR):
                m, l, acc = states[n]
                po[c * CELL + i, :, n * HD:(n + 1) * HD] = (acc / l).astype(jnp.bfloat16)
                stats = jnp.where(lane == i * PAIR + n, m, stats)
                stats = jnp.where(lane == i * PAIR + n + HD // 2, l, stats)
            partial_copy(c * CELL + i).start()
            return stats

        ps[c] = lax.fori_loop(0, CELL, serve, jnp.zeros((rows, HD), jnp.float32))
        stats_copy(c).start()

    def finish(i):
        states = list(memory_states(cell * CELL + i))
        for c in range(cells - 1):
            if c == 0:

                @pl.when(i == 0)
                def _():
                    each(0, cells - 1, lambda x: stats_copy(x).wait_recv())

            partial_copy(c * CELL + i).wait_recv()
            there = rs[c]
            for n in range(PAIR):
                m, l, acc = states[n]
                m_far = jnp.sum(jnp.where(lane == i * PAIR + n, there, 0.0), axis=-1, keepdims=True)
                l_far = jnp.sum(jnp.where(lane == i * PAIR + n + HD // 2, there, 0.0), axis=-1, keepdims=True)
                top = jnp.maximum(m, m_far)
                w = jnp.exp2((m - top) * SCALE2)
                w_far = jnp.exp2((m_far - top) * SCALE2) * l_far
                far = ro[c * CELL + i, :, n * HD:(n + 1) * HD].astype(jnp.float32)
                states[n] = (top, l * w + w_far, acc * w + far * w_far)
        for n in range(PAIR):
            m, l, acc = states[n]
            memory = (acc / l).astype(jnp.bfloat16).astype(jnp.float32)
            context = ctx[i, :, n * HD:(n + 1) * HD].astype(jnp.float32)
            gate = gate_ref[spot * PAIR + n]
            os[i, :, n * HD:(n + 1) * HD] = (gate * memory + (1.0 - gate) * context).astype(jnp.bfloat16)

        @pl.when(i == spot)
        def _():
            result_self().start()

        @pl.when(i != spot)
        def _():
            result_copy(i).start()

    each(0, CELL, finish)

    result_self().wait()
    each(1, CELL, lambda step: result_arrival((spot + step) % CELL).wait_recv())
    each(1, CELL, lambda step: result_copy((spot + step) % CELL).wait_send())
    each(1, size, lambda step: table_copy(step).wait_send())
    each(1, size, lambda step: query_copy((me + step) % size).wait_send())

    def drain_context(step):
        other = (chip + step) % chips

        @pl.when(other // KVH >= cell)
        def _():
            for copy in context_copies(other):
                copy.wait_send()

    each(1, chips, drain_context)

    def drain_forward(other):
        for copy in context_forwards(other * 2 + core):
            copy.wait_send()

    each(0, (cell + 1) * KVH, drain_forward)

    def drain_store(step):
        for copy in store_copies((head + step) % KVH):
            copy.wait_send()

    each(1, KVH, drain_store)

    def drain_store_forward(other):
        for copy in store_forwards(other * 2 + core):
            copy.wait_send()

    each(0, KVH, drain_store_forward)
    each(0, (cells - 1) * CELL, lambda slot: partial_copy(slot).wait_send())
    each(0, cells - 1, lambda c: stats_copy(c).wait_send())


def attention_call(gate, table, queries, keys, values, store_keys, store_values, size):
    rows = queries.shape[0]
    cells = size // CELL
    chips = size // 2
    local = store_keys.shape[0]
    far = max(cells - 1, 1)
    block = (rows, WIDTH)
    dma = pltpu.SemaphoreType.DMA
    return pl.pallas_call(
        functools.partial(attention_kernel, size, size * CAP != TOPM),
        out_shape=jax.ShapeDtypeStruct(queries.shape, jnp.bfloat16),
        in_specs=[pl.BlockSpec(memory_space=pltpu.SMEM)] + [pl.BlockSpec(memory_space=pl.ANY)] * 6,
        out_specs=pl.BlockSpec(memory_space=pltpu.VMEM),
        scratch_shapes=[
            pltpu.SMEM((size, HD), jnp.int32),
            pltpu.VMEM((size, *block), jnp.bfloat16),
            pltpu.VMEM((size, rows, HD), jnp.bfloat16),
            pltpu.VMEM((size, rows, HD), jnp.bfloat16),
            pltpu.VMEM((CELL * local, MROWS, HD), jnp.bfloat16),
            pltpu.VMEM((CELL * local, MROWS, HD), jnp.bfloat16),
            pltpu.VMEM((CELL, *block), jnp.bfloat16),
            pltpu.VMEM((far * CELL, *block), jnp.bfloat16),
            pltpu.VMEM((far * CELL, *block), jnp.bfloat16),
            pltpu.VMEM((far, rows, HD), jnp.float32),
            pltpu.VMEM((far, rows, HD), jnp.float32),
            pltpu.VMEM((CELL, *block), jnp.bfloat16),
            dma((2, size)),
            dma((2, size)),
            dma((2, chips)),
            dma((2, size)),
            dma((2, chips)),
            dma((2, KVH)),
            dma((2, CELL)),
            dma((2, KVH)),
            dma((2, far * CELL)),
            dma((2, far)),
            dma((2, CELL)),
            dma((7,)),
        ],
        compiler_params=pltpu.CompilerParams(
            collective_id=0, has_side_effects=True, vmem_limit_bytes=VMEM_LIMIT
        ),
        cost_estimate=pl.CostEstimate(
            flops=16 * 4096 * 256 * 512, bytes_accessed=20_000_000, transcendentals=16 * 4096 * 256
        ),
    )(gate, table, queries, keys, values, store_keys, store_values)


def on_device(
    queries, ctx_keys, ctx_values, store_keys, store_values, block_ids, block_slot, gate_logit
):
    size = lax.axis_size("seq")
    local_count = store_keys.shape[0]
    my_slots = lookup_slots(block_ids.reshape(-1), block_slot)
    my_table = request_table(my_slots, size, CAP, local_count).reshape(-1)
    table = jnp.pad(my_table, (0, HD - size * CAP))
    gate = jax.nn.sigmoid(gate_logit)
    return attention_call(gate, table, queries, ctx_keys, ctx_values, store_keys, store_values, size)


def solution(mesh):
    placed = (
        P(("groups", "seq"), None),
        P(("groups", "seq"), None),
        P(("groups", "seq"), None),
        P(("groups", "seq"), None, None),
        P(("groups", "seq"), None, None),
        P(("groups", "seq"), None),
        P("groups"),
        P(),
    )
    return jax.shard_map(
        on_device, mesh=mesh, in_specs=placed, out_specs=P(("groups", "seq"), None), check_vma=False
    )
```

```python
import functools

import jax
import jax.numpy as jnp
from jax import lax
from jax.experimental import pallas as pl
from jax.experimental.pallas import tpu as pltpu
from jax.sharding import PartitionSpec as P

H = 16
KVH = 4
HD = 128
GROUP = H // KVH
QBLK = 256
MROWS = 128
TOPM = 32
CAP = 2
CELL = 2 * KVH
PAIR = 2
WIDTH = PAIR * HD
TILE = 1024
SPAN = CELL * QBLK // TILE
PICKS = CELL * CAP
PER_TILE = TILE // MROWS
HALF = CELL // 2
STATS = 2 * HALF * PAIR

NEG = -1e30
SCALE2 = HD ** (-0.5) * 1.4426950408889634
VMEM_LIMIT = 60 * 1024 * 1024
MESH = pl.DeviceIdType.MESH


def request_table(slots, owners_count, capacity, local_count):
    entries = slots.shape[0]
    owner = slots // local_count
    local = slots % local_count
    order = jnp.arange(entries, dtype=jnp.int32)
    earlier = (owner[:, None] == owner[None, :]) & (order[None, :] < order[:, None])
    rank = jnp.sum(earlier.astype(jnp.int32), axis=1)
    chosen = (owner[:, None, None] == jnp.arange(owners_count, dtype=jnp.int32)[None, :, None]) & (
        rank[:, None, None] == jnp.arange(capacity, dtype=jnp.int32)[None, None, :]
    )
    return jnp.sum(jnp.where(chosen, local[:, None, None] + 1, 0), axis=0) - 1


def lookup_slots(wanted_ids, block_slot):
    hits = wanted_ids[..., None] == jnp.arange(block_slot.shape[0], dtype=jnp.int32)
    return jnp.sum(jnp.where(hits, block_slot, 0), axis=-1)


def fresh(rows):
    return (
        jnp.full((rows, 1), NEG, jnp.float32),
        jnp.zeros((rows, 1), jnp.float32),
        jnp.zeros((rows, HD), jnp.float32),
    )


def scores(q, k):
    return lax.dot_general(q, k, (((1,), (1,)), ((), ())), preferred_element_type=jnp.float32)


def absorb(state, s, v):
    if state is None:
        m = jnp.max(s, axis=-1, keepdims=True)
        p = jnp.exp2((s - m) * SCALE2)
        l = jnp.sum(p, axis=-1, keepdims=True)
        return m, l, jnp.dot(p.astype(jnp.bfloat16), v, preferred_element_type=jnp.float32)
    m, l, acc = state
    m_new = jnp.maximum(m, jnp.max(s, axis=-1, keepdims=True))
    decay = jnp.exp2((m - m_new) * SCALE2)
    p = jnp.exp2((s - m_new) * SCALE2)
    l = l * decay + jnp.sum(p, axis=-1, keepdims=True)
    acc = acc * decay + jnp.dot(p.astype(jnp.bfloat16), v, preferred_element_type=jnp.float32)
    return m_new, l, acc


def run_steps(states, steps):
    states = list(states)
    ahead = scores(*steps[0][1:3])
    for n, (head, _, _, v, change) in enumerate(steps):
        s = ahead
        if n + 1 < len(steps):
            ahead = scores(*steps[n + 1][1:3])
        if change is not None:
            s = change(s)
        states[head] = absorb(states[head], s, v)
    return tuple(states)


def attention_kernel(size, masked, gate_ref, table_ref, q_ref, key_ref, value_ref, sk_ref, sv_ref, out_ref,
                     tb, qs, ck, cv, sk, sv, om, ol, oa, po, ro, ps, rs, rt, os,
                     t_sem, q_sem, kv_send, kv_recv, kv_fwd, st_send, st_recv, st_fwd,
                     po_sem, ps_sem, out_sem, self_sem):
    cells = size // CELL
    chips = size // 2
    me = lax.axis_index("seq")
    cell = me // CELL
    spot = me % CELL
    chip = me // 2
    head = chip % KVH
    core = me % 2
    peer = chip * 2 + 1 - core
    inner = 1 - 2 * cell // cells
    rows = q_ref.shape[0]
    local = sk_ref.shape[0]

    def lanes_of(j, width):
        return pl.ds(pl.multiple_of(j * width, width), width)

    def remote(src, dst, send, recv, device):
        return pltpu.make_async_remote_copy(
            src_ref=src, dst_ref=dst, send_sem=send, recv_sem=recv,
            device_id={"seq": device}, device_id_type=MESH,
        )

    def table_copy(step):
        return remote(table_ref, tb.at[me], t_sem.at[0, step], t_sem.at[1, me], (me + step) % size)

    def table_arrival(step):
        return remote(table_ref, tb.at[(me + step) % size], t_sem.at[0, step], t_sem.at[1, (me + step) % size], peer)

    def query_copy(device):
        return remote(q_ref.at[:, lanes_of(device % CELL, WIDTH)], qs.at[me],
                      q_sem.at[0, device], q_sem.at[1, me], device)

    def query_arrival(device):
        return remote(qs.at[device], qs.at[device], q_sem.at[0, device], q_sem.at[1, device], peer)

    def context_copies(other):
        return tuple(
            remote(src.at[:, lanes_of(other % KVH, HD)], dst.at[me],
                   kv_send.at[w, other], kv_recv.at[w, me], other * 2 + core)
            for w, (src, dst) in enumerate(((key_ref, ck), (value_ref, cv)))
        )

    def context_forwards(source):
        return tuple(
            remote(buf.at[source], buf.at[source], kv_fwd.at[w, source // 2], kv_recv.at[w, source], peer)
            for w, buf in enumerate((ck, cv))
        )

    def owned(o):
        return pl.ds(pl.multiple_of(o * local, local), local)

    def store_copies(other):
        return tuple(
            remote(src.at[:, :, lanes_of(other, HD)], dst.at[owned(spot)],
                   st_send.at[w, other], st_recv.at[w, spot], cell * CELL + other * 2 + core)
            for w, (src, dst) in enumerate(((sk_ref, sk), (sv_ref, sv)))
        )

    def store_forwards(o):
        return tuple(
            remote(buf.at[owned(o)], buf.at[owned(o)], st_fwd.at[w, o // 2], st_recv.at[w, o], peer)
            for w, buf in enumerate((sk, sv))
        )

    def self_copies():
        return (
            pltpu.make_async_copy(table_ref, tb.at[me], self_sem.at[0]),
            pltpu.make_async_copy(q_ref.at[:, lanes_of(spot, WIDTH)], qs.at[me], self_sem.at[1]),
            pltpu.make_async_copy(key_ref.at[:, lanes_of(head, HD)], ck.at[me], self_sem.at[2]),
            pltpu.make_async_copy(value_ref.at[:, lanes_of(head, HD)], cv.at[me], self_sem.at[3]),
            pltpu.make_async_copy(sk_ref.at[:, :, lanes_of(head, HD)], sk.at[owned(spot)], self_sem.at[4]),
            pltpu.make_async_copy(sv_ref.at[:, :, lanes_of(head, HD)], sv.at[owned(spot)], self_sem.at[5]),
        )

    def partial_copy(slot):
        away = (cell + 1 + slot // CELL) % cells
        return remote(po.at[slot], ro.at[slot], po_sem.at[0, slot], po_sem.at[1, slot], away * CELL + spot)

    def stats_copy(x):
        return remote(ps.at[x], rs.at[x], ps_sem.at[0, x], ps_sem.at[1, x], (cell + 1 + x // 2) % cells * CELL + spot)

    def result_copy(i):
        return remote(os.at[i], out_ref.at[:, lanes_of(spot, WIDTH)],
                      out_sem.at[0, i], out_sem.at[1, spot], cell * CELL + i)

    def result_arrival(u):
        return remote(os.at[0], out_ref.at[:, lanes_of(u, WIDTH)], out_sem.at[0, u], out_sem.at[1, u], peer)

    def result_self():
        return pltpu.make_async_copy(os.at[spot], out_ref.at[:, lanes_of(spot, WIDTH)], self_sem.at[6])

    def each(low, high, body):
        def step(i, carry):
            body(i)
            return carry

        lax.fori_loop(low, high, step, 0)

    def start(*copies):
        for copy in copies:
            copy.start()

    mine = self_copies()
    start(*mine)

    barrier = pltpu.get_barrier_semaphore()
    each(1, size, lambda step: pl.semaphore_signal(
        barrier, inc=1, device_id={"seq": (me + step) % size}, device_id_type=MESH))
    pl.semaphore_wait(barrier, size - 1)

    def far_device(step):
        return (cell * CELL + step // CELL * CELL + (spot + step) % CELL) % size

    def near_device(step):
        plane = (spot // HALF + step // HALF) % 2
        return cell * CELL + plane * HALF + (spot + step) % HALF

    def send_context(step):
        other = (chip + step) % chips

        @pl.when(other // KVH >= cell)
        def _():
            start(*context_copies(other))

    def send_far():
        each(CELL, size, lambda step: query_copy(far_device(step)).start())

    def send_far_context():
        each(KVH, chips, lambda step: send_context((cell * KVH + step - chip) % chips))

    def send_near_context():
        each(1, KVH, lambda step: send_context((cell * KVH + (head + step) % KVH - chip) % chips))

    close = spot // HALF == inner
    each(1, size, lambda step: table_copy(step).start())

    @pl.when(close)
    def _():
        send_far()

    each(1, KVH, lambda step: start(*store_copies((head + step) % KVH)))
    each(1, HALF, lambda step: query_copy(near_device(step)).start())

    @pl.when(close)
    def _():
        send_far_context()

    mine[4].wait()
    mine[5].wait()
    start(*store_forwards(spot))

    def drain_store(step):
        for copy in store_copies((head + step) % KVH):
            copy.wait_send()

    each(1, KVH, drain_store)

    @pl.when(jnp.logical_not(close))
    def _():
        send_far()

    each(HALF, CELL, lambda step: query_copy(near_device(step)).start())

    @pl.when(jnp.logical_not(close))
    def _():
        send_far_context()

    send_near_context()
    mine[2].wait()
    mine[3].wait()
    start(*context_forwards(me))

    def relay_store(step):
        o = (head + step) % KVH * 2 + core
        for copy in store_forwards(o):
            copy.wait_recv()
        start(*store_forwards(o))

    each(1, KVH, relay_store)

    def arrive_store(other):
        for copy in store_forwards(other * 2 + 1 - core):
            copy.wait_recv()

    each(0, KVH, arrive_store)
    mine[0].wait()
    each(1, size, lambda step: table_arrival(step).wait_recv())

    def head_of(b, n):
        return qs[b, :, n * HD:(n + 1) * HD]

    def context_tile(t):
        at = pl.ds(t * (TILE // QBLK), TILE // QBLK)
        return ck[at].reshape(TILE, HD), cv[at].reshape(TILE, HD)

    def context_query(i):
        late = i // HALF
        q = [head_of(cell * CELL + i, n) for n in range(PAIR)]
        spots = i % HALF * rows + lax.broadcasted_iota(jnp.int32, (rows, TILE), 0)
        allowed = lax.broadcasted_iota(jnp.int32, (rows, TILE), 1) <= spots

        def causal(s):
            return jnp.where(allowed, s, NEG)

        def tile_steps(t, change):
            k, v = context_tile(t)
            return [(n, q[n], k, v, change) for n in range(PAIR)]

        def before(t, states):
            return run_steps(states, tile_steps(cell * SPAN + t, None))

        def earlier(c, states):
            return run_steps(states, sum((tile_steps(c * SPAN + t, None) for t in range(SPAN)), []))

        states = run_steps((None, None), tile_steps(cell * SPAN + late, causal))
        states = lax.fori_loop(0, late, before, states)
        return lax.fori_loop(0, cell, earlier, states)

    lane = lax.broadcasted_iota(jnp.int32, (rows, HD), 1)

    def memory_states(b):
        q = [head_of(b, n) for n in range(PAIR)]
        steps = []
        for t in range(PICKS // PER_TILE):
            ks, vs, gone = [], [], []
            for x in range(PER_TILE):
                pick = t * PER_TILE + x
                there = tb[b, cell * PICKS + pick]
                at = pick // CAP * local + jnp.maximum(there, 0)
                ks.append(sk[at])
                vs.append(sv[at])
                gone.append(jnp.where(there < 0, NEG, 0.0).astype(jnp.float32))
            k, v = jnp.concatenate(ks, axis=0), jnp.concatenate(vs, axis=0)

            def hide(s, gone=gone):
                return jnp.concatenate(
                    [s[:, x * MROWS:(x + 1) * MROWS] + gone[x] for x in range(PER_TILE)], axis=1
                )

            steps += [(n, q[n], k, v, hide if masked else None) for n in range(PAIR)]
        return run_steps((None, None), steps)

    def serve_half(c, part):
        away = (cell + 1 + c) % cells
        first = ((cell - away + cells - 1) // cells + part) % 2 * HALF

        def serve(k, stats):
            b = away * CELL + first + k
            query_arrival(b).wait_recv()
            states = memory_states(b)
            slot = c * CELL + first + k
            for n in range(PAIR):
                m, l, acc = states[n]
                po[slot, :, n * HD:(n + 1) * HD] = (acc / l).astype(jnp.bfloat16)
                stats = jnp.where(lane == k * PAIR + n, m, stats)
                stats = jnp.where(lane == k * PAIR + n + STATS // 2, l, stats)
            partial_copy(slot).start()
            return stats

        stats = lax.fori_loop(0, HALF, serve, jnp.zeros((rows, HD), jnp.float32))
        ps[c * 2 + part] = stats.T[:STATS]
        stats_copy(c * 2 + part).start()

    def remember(step):
        b = near_device(step)
        i = b - cell * CELL

        @pl.when(step > 0)
        def _():
            query_arrival(b).wait_recv()

        for n, (m, l, acc) in enumerate(memory_states(b)):
            om[i, n] = m
            ol[i, n] = l
            oa[i, n] = acc

    for c in range(cells - 1):
        serve_half(c, 0)
    mine[1].wait()
    each(0, HALF, remember)
    each(HALF, CELL, remember)
    for c in range(cells - 1):
        serve_half(c, 1)

    def relay_context(step):
        other = (chip + step) % chips

        @pl.when(other // KVH <= cell)
        def _():
            for copy in context_forwards(other * 2 + core):
                copy.wait_recv()
            start(*context_forwards(other * 2 + core))

    each(1, chips, relay_context)

    def arrive_context(other):
        for copy in context_forwards(other * 2 + 1 - core):
            copy.wait_recv()

    each(0, (cell + 1) * KVH, arrive_context)

    def finish(k, part):
        i = (inner + part) % 2 * HALF + k
        near = context_query(i)
        for c in range(cells - 1):
            partial_copy(c * CELL + i).wait_recv()
        for n in range(PAIR):
            m, l, acc = om[i, n], ol[i, n], oa[i, n]
            for c in range(cells - 1):
                there = rt[c * 2 + part]
                m_far = jnp.sum(jnp.where(lane == k * PAIR + n, there, 0.0), axis=-1, keepdims=True)
                l_far = jnp.sum(jnp.where(lane == k * PAIR + n + STATS // 2, there, 0.0), axis=-1, keepdims=True)
                top = jnp.maximum(m, m_far)
                w = jnp.exp2((m - top) * SCALE2)
                w_far = jnp.exp2((m_far - top) * SCALE2) * l_far
                far = ro[c * CELL + i, :, n * HD:(n + 1) * HD].astype(jnp.float32)
                m, l, acc = top, l * w + w_far, acc * w + far * w_far
            memory = (acc / l).astype(jnp.bfloat16).astype(jnp.float32)
            context = (near[n][2] / near[n][1]).astype(jnp.bfloat16).astype(jnp.float32)
            gate = gate_ref[spot * PAIR + n]
            os[i, :, n * HD:(n + 1) * HD] = (gate * memory + (1.0 - gate) * context).astype(jnp.bfloat16)

        @pl.when(i == spot)
        def _():
            result_self().start()

        @pl.when(i != spot)
        def _():
            result_copy(i).start()

    for part in range(2):
        for c in range(cells - 1):
            x = c * 2 + part
            stats_copy(x).wait_recv()
            rt[x] = jnp.concatenate([rs[x], jnp.zeros((HD - STATS, rows), jnp.float32)], axis=0).T
        each(0, HALF, lambda k, part=part: finish(k, part))

    result_self().wait()
    each(1, CELL, lambda step: result_arrival((spot + step) % CELL).wait_recv())
    each(1, CELL, lambda step: result_copy((spot + step) % CELL).wait_send())
    each(1, size, lambda step: table_copy(step).wait_send())
    each(1, size, lambda step: query_copy((me + step) % size).wait_send())

    def drain_context(step):
        other = (chip + step) % chips

        @pl.when(other // KVH >= cell)
        def _():
            for copy in context_copies(other):
                copy.wait_send()

    each(1, chips, drain_context)

    def drain_forward(other):
        for copy in context_forwards(other * 2 + core):
            copy.wait_send()

    each(0, (cell + 1) * KVH, drain_forward)

    def drain_store_forward(other):
        for copy in store_forwards(other * 2 + core):
            copy.wait_send()

    each(0, KVH, drain_store_forward)
    each(0, (cells - 1) * CELL, lambda slot: partial_copy(slot).wait_send())
    each(0, 2 * (cells - 1), lambda x: stats_copy(x).wait_send())


def attention_call(gate, table, queries, keys, values, store_keys, store_values, size):
    rows = queries.shape[0]
    cells = size // CELL
    chips = size // 2
    local = store_keys.shape[0]
    far = max(cells - 1, 1)
    block = (rows, WIDTH)
    dma = pltpu.SemaphoreType.DMA
    return pl.pallas_call(
        functools.partial(attention_kernel, size, size * CAP != TOPM),
        out_shape=jax.ShapeDtypeStruct(queries.shape, jnp.bfloat16),
        in_specs=[pl.BlockSpec(memory_space=pltpu.SMEM)] + [pl.BlockSpec(memory_space=pl.ANY)] * 6,
        out_specs=pl.BlockSpec(memory_space=pltpu.VMEM),
        scratch_shapes=[
            pltpu.SMEM((size, HD), jnp.int32),
            pltpu.VMEM((size, *block), jnp.bfloat16),
            pltpu.VMEM((size, rows, HD), jnp.bfloat16),
            pltpu.VMEM((size, rows, HD), jnp.bfloat16),
            pltpu.VMEM((CELL * local, MROWS, HD), jnp.bfloat16),
            pltpu.VMEM((CELL * local, MROWS, HD), jnp.bfloat16),
            pltpu.VMEM((CELL, PAIR, rows, 1), jnp.float32),
            pltpu.VMEM((CELL, PAIR, rows, 1), jnp.float32),
            pltpu.VMEM((CELL, PAIR, rows, HD), jnp.float32),
            pltpu.VMEM((far * CELL, *block), jnp.bfloat16),
            pltpu.VMEM((far * CELL, *block), jnp.bfloat16),
            pltpu.VMEM((2 * far, STATS, rows), jnp.float32),
            pltpu.VMEM((2 * far, STATS, rows), jnp.float32),
            pltpu.VMEM((2 * far, rows, HD), jnp.float32),
            pltpu.VMEM((CELL, *block), jnp.bfloat16),
            dma((2, size)),
            dma((2, size)),
            dma((2, chips)),
            dma((2, size)),
            dma((2, chips)),
            dma((2, KVH)),
            dma((2, CELL)),
            dma((2, KVH)),
            dma((2, far * CELL)),
            dma((2, 2 * far)),
            dma((2, CELL)),
            dma((7,)),
        ],
        compiler_params=pltpu.CompilerParams(
            collective_id=0, has_side_effects=True, vmem_limit_bytes=VMEM_LIMIT
        ),
        cost_estimate=pl.CostEstimate(
            flops=16 * 4096 * 256 * 512, bytes_accessed=20_000_000, transcendentals=16 * 4096 * 256
        ),
    )(gate, table, queries, keys, values, store_keys, store_values)


def on_device(
    queries, ctx_keys, ctx_values, store_keys, store_values, block_ids, block_slot, gate_logit
):
    size = lax.axis_size("seq")
    local_count = store_keys.shape[0]
    my_slots = lookup_slots(block_ids.reshape(-1), block_slot)
    my_table = request_table(my_slots, size, CAP, local_count).reshape(-1)
    table = jnp.pad(my_table, (0, HD - size * CAP))
    gate = jax.nn.sigmoid(gate_logit)
    return attention_call(gate, table, queries, ctx_keys, ctx_values, store_keys, store_values, size)


def solution(mesh):
    placed = (
        P(("groups", "seq"), None),
        P(("groups", "seq"), None),
        P(("groups", "seq"), None),
        P(("groups", "seq"), None, None),
        P(("groups", "seq"), None, None),
        P(("groups", "seq"), None),
        P("groups"),
        P(),
    )
    return jax.shard_map(
        on_device, mesh=mesh, in_specs=placed, out_specs=P(("groups", "seq"), None), check_vma=False
    )
```

```python
import functools

import jax
import jax.numpy as jnp
from jax import lax
from jax.experimental import pallas as pl
from jax.experimental.pallas import tpu as pltpu
from jax.sharding import PartitionSpec as P

H = 16
KVH = 4
HD = 128
GROUP = H // KVH
QBLK = 256
MROWS = 128
TOPM = 32
CAP = 2
CELL = 2 * KVH
PAIR = 2
WIDTH = PAIR * HD
TILE = 1024
SPAN = CELL * QBLK // TILE
PICKS = CELL * CAP
PER_TILE = TILE // MROWS
HALF = CELL // 2
STATS = 2 * HALF * PAIR

NEG = -1e30
SCALE2 = HD ** (-0.5) * 1.4426950408889634
VMEM_LIMIT = 60 * 1024 * 1024
MESH = pl.DeviceIdType.MESH


def request_table(slots, owners_count, capacity, local_count):
    entries = slots.shape[0]
    owner = slots // local_count
    local = slots % local_count
    order = jnp.arange(entries, dtype=jnp.int32)
    earlier = (owner[:, None] == owner[None, :]) & (order[None, :] < order[:, None])
    rank = jnp.sum(earlier.astype(jnp.int32), axis=1)
    chosen = (owner[:, None, None] == jnp.arange(owners_count, dtype=jnp.int32)[None, :, None]) & (
        rank[:, None, None] == jnp.arange(capacity, dtype=jnp.int32)[None, None, :]
    )
    return jnp.sum(jnp.where(chosen, local[:, None, None] + 1, 0), axis=0) - 1


def lookup_slots(wanted_ids, block_slot):
    hits = wanted_ids[..., None] == jnp.arange(block_slot.shape[0], dtype=jnp.int32)
    return jnp.sum(jnp.where(hits, block_slot, 0), axis=-1)


def fresh(rows):
    return (
        jnp.full((rows, 1), NEG, jnp.float32),
        jnp.zeros((rows, 1), jnp.float32),
        jnp.zeros((rows, HD), jnp.float32),
    )


def scores(q, k):
    return lax.dot_general(q, k, (((1,), (1,)), ((), ())), preferred_element_type=jnp.float32)


def absorb(state, s, v):
    if state is None:
        m = jnp.max(s, axis=-1, keepdims=True)
        p = jnp.exp2((s - m) * SCALE2)
        l = jnp.sum(p, axis=-1, keepdims=True)
        return m, l, jnp.dot(p.astype(jnp.bfloat16), v, preferred_element_type=jnp.float32)
    m, l, acc = state
    m_new = jnp.maximum(m, jnp.max(s, axis=-1, keepdims=True))
    decay = jnp.exp2((m - m_new) * SCALE2)
    p = jnp.exp2((s - m_new) * SCALE2)
    l = l * decay + jnp.sum(p, axis=-1, keepdims=True)
    acc = acc * decay + jnp.dot(p.astype(jnp.bfloat16), v, preferred_element_type=jnp.float32)
    return m_new, l, acc


def run_steps(states, steps):
    states = list(states)
    ahead = scores(*steps[0][1:3])
    for n, (head, _, _, v, change) in enumerate(steps):
        s = ahead
        if n + 1 < len(steps):
            ahead = scores(*steps[n + 1][1:3])
        if change is not None:
            s = change(s)
        states[head] = absorb(states[head], s, v)
    return tuple(states)


def attention_kernel(size, masked, gate_ref, table_ref, q_ref, key_ref, value_ref, sk_ref, sv_ref, out_ref,
                     tb, qs, ck, cv, sk, sv, om, ol, oa, po, ro, ps, rs, rt, os,
                     t_sem, q_sem, kv_send, kv_recv, kv_fwd, st_send, st_recv, st_fwd,
                     po_sem, ps_sem, out_sem, self_sem):
    cells = size // CELL
    chips = size // 2
    me = lax.axis_index("seq")
    cell = me // CELL
    spot = me % CELL
    chip = me // 2
    head = chip % KVH
    core = me % 2
    peer = chip * 2 + 1 - core
    inner = 1 - 2 * cell // cells
    rows = q_ref.shape[0]
    local = sk_ref.shape[0]

    def lanes_of(j, width):
        return pl.ds(pl.multiple_of(j * width, width), width)

    def remote(src, dst, send, recv, device):
        return pltpu.make_async_remote_copy(
            src_ref=src, dst_ref=dst, send_sem=send, recv_sem=recv,
            device_id={"seq": device}, device_id_type=MESH,
        )

    def table_copy(step):
        return remote(table_ref, tb.at[me], t_sem.at[0, step], t_sem.at[1, me], (me + step) % size)

    def table_arrival(step):
        return remote(table_ref, tb.at[(me + step) % size], t_sem.at[0, step], t_sem.at[1, (me + step) % size], peer)

    def query_copy(device):
        return remote(q_ref.at[:, lanes_of(device % CELL, WIDTH)], qs.at[me],
                      q_sem.at[0, device], q_sem.at[1, me], device)

    def query_arrival(device):
        return remote(qs.at[device], qs.at[device], q_sem.at[0, device], q_sem.at[1, device], peer)

    def context_copies(other):
        return tuple(
            remote(src.at[:, lanes_of(other % KVH, HD)], dst.at[me],
                   kv_send.at[w, other], kv_recv.at[w, me], other * 2 + core)
            for w, (src, dst) in enumerate(((key_ref, ck), (value_ref, cv)))
        )

    def context_forwards(source):
        return tuple(
            remote(buf.at[source], buf.at[source], kv_fwd.at[w, source // 2], kv_recv.at[w, source], peer)
            for w, buf in enumerate((ck, cv))
        )

    def owned(o):
        return pl.ds(pl.multiple_of(o * local, local), local)

    def store_copies(other):
        return tuple(
            remote(src.at[:, :, lanes_of(other, HD)], dst.at[owned(spot)],
                   st_send.at[w, other], st_recv.at[w, spot], cell * CELL + other * 2 + core)
            for w, (src, dst) in enumerate(((sk_ref, sk), (sv_ref, sv)))
        )

    def store_forwards(o):
        return tuple(
            remote(buf.at[owned(o)], buf.at[owned(o)], st_fwd.at[w, o // 2], st_recv.at[w, o], peer)
            for w, buf in enumerate((sk, sv))
        )

    def self_copies():
        return (
            pltpu.make_async_copy(table_ref, tb.at[me], self_sem.at[0]),
            pltpu.make_async_copy(q_ref.at[:, lanes_of(spot, WIDTH)], qs.at[me], self_sem.at[1]),
            pltpu.make_async_copy(key_ref.at[:, lanes_of(head, HD)], ck.at[me], self_sem.at[2]),
            pltpu.make_async_copy(value_ref.at[:, lanes_of(head, HD)], cv.at[me], self_sem.at[3]),
            pltpu.make_async_copy(sk_ref.at[:, :, lanes_of(head, HD)], sk.at[owned(spot)], self_sem.at[4]),
            pltpu.make_async_copy(sv_ref.at[:, :, lanes_of(head, HD)], sv.at[owned(spot)], self_sem.at[5]),
        )

    def partial_copy(slot):
        away = (cell + 1 + slot // CELL) % cells
        return remote(po.at[slot], ro.at[slot], po_sem.at[0, slot], po_sem.at[1, slot], away * CELL + spot)

    def stats_copy(x):
        return remote(ps.at[x], rs.at[x], ps_sem.at[0, x], ps_sem.at[1, x], (cell + 1 + x // 2) % cells * CELL + spot)

    def result_copy(i):
        return remote(os.at[i], out_ref.at[:, lanes_of(spot, WIDTH)],
                      out_sem.at[0, i], out_sem.at[1, spot], cell * CELL + i)

    def result_arrival(u):
        return remote(os.at[0], out_ref.at[:, lanes_of(u, WIDTH)], out_sem.at[0, u], out_sem.at[1, u], peer)

    def result_self():
        return pltpu.make_async_copy(os.at[spot], out_ref.at[:, lanes_of(spot, WIDTH)], self_sem.at[6])

    def each(low, high, body):
        def step(i, carry):
            body(i)
            return carry

        lax.fori_loop(low, high, step, 0)

    def start(*copies):
        for copy in copies:
            copy.start()

    mine = self_copies()
    start(*mine)

    barrier = pltpu.get_barrier_semaphore()
    each(1, size, lambda step: pl.semaphore_signal(
        barrier, inc=1, device_id={"seq": (me + step) % size}, device_id_type=MESH))
    pl.semaphore_wait(barrier, size - 1)

    def far_device(step):
        return (cell * CELL + step // CELL * CELL + (spot + step) % CELL) % size

    def near_device(step):
        plane = (spot // HALF + step // HALF) % 2
        return cell * CELL + plane * HALF + (spot + step) % HALF

    def send_context(step):
        other = (chip + step) % chips

        @pl.when(other // KVH >= cell)
        def _():
            start(*context_copies(other))

    def send_far():
        each(CELL, size, lambda step: query_copy(far_device(step)).start())

    def send_far_context():
        each(KVH, chips, lambda step: send_context((cell * KVH + step - chip) % chips))

    def send_near_context():
        each(1, KVH, lambda step: send_context((cell * KVH + (head + step) % KVH - chip) % chips))

    close = spot // HALF == inner
    each(1, size, lambda step: table_copy(step).start())

    each(1, KVH, lambda step: start(*store_copies((head + step) % KVH)))

    @pl.when(close)
    def _():
        send_far()

    each(1, HALF, lambda step: query_copy(near_device(step)).start())

    send_far_context()

    mine[4].wait()
    mine[5].wait()
    start(*store_forwards(spot))

    def drain_store(step):
        for copy in store_copies((head + step) % KVH):
            copy.wait_send()

    each(1, KVH, drain_store)

    @pl.when(jnp.logical_not(close))
    def _():
        send_far()

    @pl.when(close)
    def _():
        each(HALF, CELL, lambda step: query_copy(near_device(step)).start())
        send_near_context()

    mine[2].wait()
    mine[3].wait()
    start(*context_forwards(me))

    def relay_store(step):
        o = (head + step) % KVH * 2 + core
        for copy in store_forwards(o):
            copy.wait_recv()
        start(*store_forwards(o))

    each(1, KVH, relay_store)

    def arrive_store(other):
        for copy in store_forwards(other * 2 + 1 - core):
            copy.wait_recv()

    each(0, KVH, arrive_store)
    @pl.when(jnp.logical_not(close))
    def _():
        each(HALF, CELL, lambda step: query_copy(near_device(step)).start())
        send_near_context()

    mine[0].wait()
    each(1, size, lambda step: table_arrival(step).wait_recv())

    def head_of(b, n):
        return qs[b, :, n * HD:(n + 1) * HD]

    def context_tile(t):
        at = pl.ds(t * (TILE // QBLK), TILE // QBLK)
        return ck[at].reshape(TILE, HD), cv[at].reshape(TILE, HD)

    def context_query(i):
        late = i // HALF
        q = [head_of(cell * CELL + i, n) for n in range(PAIR)]
        spots = i % HALF * rows + lax.broadcasted_iota(jnp.int32, (rows, TILE), 0)
        allowed = lax.broadcasted_iota(jnp.int32, (rows, TILE), 1) <= spots

        def causal(s):
            return jnp.where(allowed, s, NEG)

        def tile_steps(t, change):
            k, v = context_tile(t)
            return [(n, q[n], k, v, change) for n in range(PAIR)]

        def before(t, states):
            return run_steps(states, tile_steps(cell * SPAN + t, None))

        def earlier(c, states):
            return run_steps(states, sum((tile_steps(c * SPAN + t, None) for t in range(SPAN)), []))

        states = run_steps((None, None), tile_steps(cell * SPAN + late, causal))
        states = lax.fori_loop(0, late, before, states)
        return lax.fori_loop(0, cell, earlier, states)

    lane = lax.broadcasted_iota(jnp.int32, (rows, HD), 1)

    def memory_states(b):
        q = [head_of(b, n) for n in range(PAIR)]
        steps = []
        for t in range(PICKS // PER_TILE):
            ks, vs, gone = [], [], []
            for x in range(PER_TILE):
                pick = t * PER_TILE + x
                there = tb[b, cell * PICKS + pick]
                at = pick // CAP * local + jnp.maximum(there, 0)
                ks.append(sk[at])
                vs.append(sv[at])
                gone.append(jnp.where(there < 0, NEG, 0.0).astype(jnp.float32))
            k, v = jnp.concatenate(ks, axis=0), jnp.concatenate(vs, axis=0)

            def hide(s, gone=gone):
                return jnp.concatenate(
                    [s[:, x * MROWS:(x + 1) * MROWS] + gone[x] for x in range(PER_TILE)], axis=1
                )

            steps += [(n, q[n], k, v, hide if masked else None) for n in range(PAIR)]
        return run_steps((None, None), steps)

    def serve_half(c, part):
        away = (cell + 1 + c) % cells
        first = ((cell - away + cells - 1) // cells + part) % 2 * HALF

        def serve(k, stats):
            b = away * CELL + first + k
            query_arrival(b).wait_recv()
            states = memory_states(b)
            slot = c * CELL + first + k
            for n in range(PAIR):
                m, l, acc = states[n]
                po[slot, :, n * HD:(n + 1) * HD] = (acc / l).astype(jnp.bfloat16)
                stats = jnp.where(lane == k * PAIR + n, m, stats)
                stats = jnp.where(lane == k * PAIR + n + STATS // 2, l, stats)
            partial_copy(slot).start()
            return stats

        stats = lax.fori_loop(0, HALF, serve, jnp.zeros((rows, HD), jnp.float32))
        ps[c * 2 + part] = stats.T[:STATS]
        stats_copy(c * 2 + part).start()

    def remember(step):
        b = near_device(step)
        i = b - cell * CELL

        @pl.when(step > 0)
        def _():
            query_arrival(b).wait_recv()

        for n, (m, l, acc) in enumerate(memory_states(b)):
            om[i, n] = m
            ol[i, n] = l
            oa[i, n] = acc

    for c in range(cells - 1):
        serve_half(c, 0)
    mine[1].wait()
    each(0, HALF, remember)
    for c in range(cells - 1):
        serve_half(c, 1)
    each(HALF, CELL, remember)

    def relay_context(step):
        other = (chip + step) % chips

        @pl.when(other // KVH <= cell)
        def _():
            for copy in context_forwards(other * 2 + core):
                copy.wait_recv()
            start(*context_forwards(other * 2 + core))

    each(1, chips, relay_context)

    def arrive_context(other):
        for copy in context_forwards(other * 2 + 1 - core):
            copy.wait_recv()

    each(0, (cell + 1) * KVH, arrive_context)

    def finish(k, part):
        i = (inner + part) % 2 * HALF + k
        near = context_query(i)
        for c in range(cells - 1):
            partial_copy(c * CELL + i).wait_recv()
        for n in range(PAIR):
            m, l, acc = om[i, n], ol[i, n], oa[i, n]
            for c in range(cells - 1):
                there = rt[c * 2 + part]
                m_far = jnp.sum(jnp.where(lane == k * PAIR + n, there, 0.0), axis=-1, keepdims=True)
                l_far = jnp.sum(jnp.where(lane == k * PAIR + n + STATS // 2, there, 0.0), axis=-1, keepdims=True)
                top = jnp.maximum(m, m_far)
                w = jnp.exp2((m - top) * SCALE2)
                w_far = jnp.exp2((m_far - top) * SCALE2) * l_far
                far = ro[c * CELL + i, :, n * HD:(n + 1) * HD].astype(jnp.float32)
                m, l, acc = top, l * w + w_far, acc * w + far * w_far
            memory = (acc / l).astype(jnp.bfloat16).astype(jnp.float32)
            context = (near[n][2] / near[n][1]).astype(jnp.bfloat16).astype(jnp.float32)
            gate = gate_ref[spot * PAIR + n]
            os[i, :, n * HD:(n + 1) * HD] = (gate * memory + (1.0 - gate) * context).astype(jnp.bfloat16)

        @pl.when(i == spot)
        def _():
            result_self().start()

        @pl.when(i != spot)
        def _():
            result_copy(i).start()

    for part in range(2):
        for c in range(cells - 1):
            x = c * 2 + part
            stats_copy(x).wait_recv()
            rt[x] = jnp.concatenate([rs[x], jnp.zeros((HD - STATS, rows), jnp.float32)], axis=0).T
        each(0, HALF, lambda k, part=part: finish(k, part))

    result_self().wait()
    each(1, CELL, lambda step: result_arrival((spot + step) % CELL).wait_recv())
    each(1, CELL, lambda step: result_copy((spot + step) % CELL).wait_send())
    each(1, size, lambda step: table_copy(step).wait_send())
    each(1, size, lambda step: query_copy((me + step) % size).wait_send())

    def drain_context(step):
        other = (chip + step) % chips

        @pl.when(other // KVH >= cell)
        def _():
            for copy in context_copies(other):
                copy.wait_send()

    each(1, chips, drain_context)

    def drain_forward(other):
        for copy in context_forwards(other * 2 + core):
            copy.wait_send()

    each(0, (cell + 1) * KVH, drain_forward)

    def drain_store_forward(other):
        for copy in store_forwards(other * 2 + core):
            copy.wait_send()

    each(0, KVH, drain_store_forward)
    each(0, (cells - 1) * CELL, lambda slot: partial_copy(slot).wait_send())
    each(0, 2 * (cells - 1), lambda x: stats_copy(x).wait_send())


def attention_call(gate, table, queries, keys, values, store_keys, store_values, size):
    rows = queries.shape[0]
    cells = size // CELL
    chips = size // 2
    local = store_keys.shape[0]
    far = max(cells - 1, 1)
    block = (rows, WIDTH)
    dma = pltpu.SemaphoreType.DMA
    return pl.pallas_call(
        functools.partial(attention_kernel, size, size * CAP != TOPM),
        out_shape=jax.ShapeDtypeStruct(queries.shape, jnp.bfloat16),
        in_specs=[pl.BlockSpec(memory_space=pltpu.SMEM)] + [pl.BlockSpec(memory_space=pl.ANY)] * 6,
        out_specs=pl.BlockSpec(memory_space=pltpu.VMEM),
        scratch_shapes=[
            pltpu.SMEM((size, HD), jnp.int32),
            pltpu.VMEM((size, *block), jnp.bfloat16),
            pltpu.VMEM((size, rows, HD), jnp.bfloat16),
            pltpu.VMEM((size, rows, HD), jnp.bfloat16),
            pltpu.VMEM((CELL * local, MROWS, HD), jnp.bfloat16),
            pltpu.VMEM((CELL * local, MROWS, HD), jnp.bfloat16),
            pltpu.VMEM((CELL, PAIR, rows, 1), jnp.float32),
            pltpu.VMEM((CELL, PAIR, rows, 1), jnp.float32),
            pltpu.VMEM((CELL, PAIR, rows, HD), jnp.float32),
            pltpu.VMEM((far * CELL, *block), jnp.bfloat16),
            pltpu.VMEM((far * CELL, *block), jnp.bfloat16),
            pltpu.VMEM((2 * far, STATS, rows), jnp.float32),
            pltpu.VMEM((2 * far, STATS, rows), jnp.float32),
            pltpu.VMEM((2 * far, rows, HD), jnp.float32),
            pltpu.VMEM((CELL, *block), jnp.bfloat16),
            dma((2, size)),
            dma((2, size)),
            dma((2, chips)),
            dma((2, size)),
            dma((2, chips)),
            dma((2, KVH)),
            dma((2, CELL)),
            dma((2, KVH)),
            dma((2, far * CELL)),
            dma((2, 2 * far)),
            dma((2, CELL)),
            dma((7,)),
        ],
        compiler_params=pltpu.CompilerParams(
            collective_id=0, has_side_effects=True, vmem_limit_bytes=VMEM_LIMIT
        ),
        cost_estimate=pl.CostEstimate(
            flops=16 * 4096 * 256 * 512, bytes_accessed=20_000_000, transcendentals=16 * 4096 * 256
        ),
    )(gate, table, queries, keys, values, store_keys, store_values)


def on_device(
    queries, ctx_keys, ctx_values, store_keys, store_values, block_ids, block_slot, gate_logit
):
    size = lax.axis_size("seq")
    local_count = store_keys.shape[0]
    my_slots = lookup_slots(block_ids.reshape(-1), block_slot)
    my_table = request_table(my_slots, size, CAP, local_count).reshape(-1)
    table = jnp.pad(my_table, (0, HD - size * CAP))
    gate = jax.nn.sigmoid(gate_logit)
    return attention_call(gate, table, queries, ctx_keys, ctx_values, store_keys, store_values, size)


def solution(mesh):
    placed = (
        P(("groups", "seq"), None),
        P(("groups", "seq"), None),
        P(("groups", "seq"), None),
        P(("groups", "seq"), None, None),
        P(("groups", "seq"), None, None),
        P(("groups", "seq"), None),
        P("groups"),
        P(),
    )
    return jax.shard_map(
        on_device, mesh=mesh, in_specs=placed, out_specs=P(("groups", "seq"), None), check_vma=False
    )
```

```python
import functools

import jax
import jax.numpy as jnp
from jax import lax
from jax.experimental import pallas as pl
from jax.experimental.pallas import tpu as pltpu
from jax.sharding import PartitionSpec as P

H = 16
KVH = 4
HD = 128
GROUP = H // KVH
QBLK = 256
MROWS = 128
TOPM = 32
CAP = 2
CELL = 2 * KVH
PAIR = 2
WIDTH = PAIR * HD
TILE = 1024
SPAN = CELL * QBLK // TILE
PICKS = CELL * CAP
PER_TILE = TILE // MROWS
HALF = CELL // 2
STATS = 2 * HALF * PAIR

NEG = -1e30
SCALE2 = HD ** (-0.5) * 1.4426950408889634
VMEM_LIMIT = 60 * 1024 * 1024
MESH = pl.DeviceIdType.MESH


def request_table(slots, owners_count, local_count):
    owner = slots // local_count
    local = slots % local_count
    held = owner[None, :] == jnp.arange(owners_count, dtype=jnp.int32)[:, None]
    high = jnp.max(jnp.where(held, local[None, :], -1), axis=1)
    low = jnp.min(jnp.where(held, local[None, :], local_count), axis=1)
    return jnp.concatenate([high, jnp.where(low < high, low, -1)])


def lookup_slots(wanted_ids, block_slot):
    hits = wanted_ids[..., None] == jnp.arange(block_slot.shape[0], dtype=jnp.int32)
    return jnp.sum(jnp.where(hits, block_slot, 0), axis=-1)


def fresh(rows):
    return (
        jnp.full((rows, 1), NEG, jnp.float32),
        jnp.zeros((rows, 1), jnp.float32),
        jnp.zeros((rows, HD), jnp.float32),
    )


def scores(q, k):
    return lax.dot_general(q, k, (((1,), (1,)), ((), ())), preferred_element_type=jnp.float32)


def absorb(state, s, v):
    if state is None:
        m = jnp.max(s, axis=-1, keepdims=True)
        p = jnp.exp2((s - m) * SCALE2)
        l = jnp.sum(p, axis=-1, keepdims=True)
        return m, l, jnp.dot(p.astype(jnp.bfloat16), v, preferred_element_type=jnp.float32)
    m, l, acc = state
    m_new = jnp.maximum(m, jnp.max(s, axis=-1, keepdims=True))
    decay = jnp.exp2((m - m_new) * SCALE2)
    p = jnp.exp2((s - m_new) * SCALE2)
    l = l * decay + jnp.sum(p, axis=-1, keepdims=True)
    acc = acc * decay + jnp.dot(p.astype(jnp.bfloat16), v, preferred_element_type=jnp.float32)
    return m_new, l, acc


def run_steps(states, steps):
    states = list(states)
    ahead = scores(*steps[0][1:3])
    for n, (head, _, _, v, change) in enumerate(steps):
        s = ahead
        if n + 1 < len(steps):
            ahead = scores(*steps[n + 1][1:3])
        if change is not None:
            s = change(s)
        states[head] = absorb(states[head], s, v)
    return tuple(states)


def attention_kernel(size, masked, gate_ref, table_ref, q_ref, key_ref, value_ref, sk_ref, sv_ref, out_ref,
                     tb, qs, ck, cv, sk, sv, om, ol, oa, cm, cl, ca, po, ro, ps, rs, rt, os,
                     t_sem, q_sem, kv_send, kv_recv, kv_fwd, st_send, st_recv, st_fwd,
                     po_sem, ps_sem, out_sem, self_sem):
    cells = size // CELL
    chips = size // 2
    me = lax.axis_index("seq")
    cell = me // CELL
    spot = me % CELL
    chip = me // 2
    head = chip % KVH
    core = me % 2
    peer = chip * 2 + 1 - core
    inner = 1 - 2 * cell // cells
    rows = q_ref.shape[0]
    local = sk_ref.shape[0]

    def lanes_of(j, width):
        return pl.ds(pl.multiple_of(j * width, width), width)

    def remote(src, dst, send, recv, device):
        return pltpu.make_async_remote_copy(
            src_ref=src, dst_ref=dst, send_sem=send, recv_sem=recv,
            device_id={"seq": device}, device_id_type=MESH,
        )

    def table_copy(step):
        return remote(table_ref, tb.at[me], t_sem.at[0, step], t_sem.at[1, me], (me + step) % size)

    def table_arrival(step):
        return remote(table_ref, tb.at[(me + step) % size], t_sem.at[0, step], t_sem.at[1, (me + step) % size], peer)

    def query_copy(device):
        return remote(q_ref.at[:, lanes_of(device % CELL, WIDTH)], qs.at[me],
                      q_sem.at[0, device], q_sem.at[1, me], device)

    def query_arrival(device):
        return remote(qs.at[device], qs.at[device], q_sem.at[0, device], q_sem.at[1, device], peer)

    def context_copies(other):
        return tuple(
            remote(src.at[:, lanes_of(other % KVH, HD)], dst.at[me],
                   kv_send.at[w, other], kv_recv.at[w, me], other * 2 + core)
            for w, (src, dst) in enumerate(((key_ref, ck), (value_ref, cv)))
        )

    def context_forwards(source):
        return tuple(
            remote(buf.at[source], buf.at[source], kv_fwd.at[w, source // 2], kv_recv.at[w, source], peer)
            for w, buf in enumerate((ck, cv))
        )

    def owned(o):
        return pl.ds(pl.multiple_of(o * local, local), local)

    def store_copies(other):
        return tuple(
            remote(src.at[:, :, lanes_of(other, HD)], dst.at[owned(spot)],
                   st_send.at[w, other], st_recv.at[w, spot], cell * CELL + other * 2 + core)
            for w, (src, dst) in enumerate(((sk_ref, sk), (sv_ref, sv)))
        )

    def store_forwards(o):
        return tuple(
            remote(buf.at[owned(o)], buf.at[owned(o)], st_fwd.at[w, o // 2], st_recv.at[w, o], peer)
            for w, buf in enumerate((sk, sv))
        )

    def self_copies():
        return (
            pltpu.make_async_copy(table_ref, tb.at[me], self_sem.at[0]),
            pltpu.make_async_copy(q_ref.at[:, lanes_of(spot, WIDTH)], qs.at[me], self_sem.at[1]),
            pltpu.make_async_copy(key_ref.at[:, lanes_of(head, HD)], ck.at[me], self_sem.at[2]),
            pltpu.make_async_copy(value_ref.at[:, lanes_of(head, HD)], cv.at[me], self_sem.at[3]),
            pltpu.make_async_copy(sk_ref.at[:, :, lanes_of(head, HD)], sk.at[owned(spot)], self_sem.at[4]),
            pltpu.make_async_copy(sv_ref.at[:, :, lanes_of(head, HD)], sv.at[owned(spot)], self_sem.at[5]),
        )

    def partial_copy(slot):
        away = (cell + 1 + slot // CELL) % cells
        return remote(po.at[slot], ro.at[slot], po_sem.at[0, slot], po_sem.at[1, slot], away * CELL + spot)

    def stats_copy(x):
        return remote(ps.at[x], rs.at[x], ps_sem.at[0, x], ps_sem.at[1, x], (cell + 1 + x // 2) % cells * CELL + spot)

    def result_copy(i):
        return remote(os.at[i], out_ref.at[:, lanes_of(spot, WIDTH)],
                      out_sem.at[0, i], out_sem.at[1, spot], cell * CELL + i)

    def result_arrival(u):
        return remote(os.at[0], out_ref.at[:, lanes_of(u, WIDTH)], out_sem.at[0, u], out_sem.at[1, u], peer)

    def result_self():
        return pltpu.make_async_copy(os.at[spot], out_ref.at[:, lanes_of(spot, WIDTH)], self_sem.at[6])

    def each(low, high, body):
        def step(i, carry):
            body(i)
            return carry

        lax.fori_loop(low, high, step, 0)

    def start(*copies):
        for copy in copies:
            copy.start()

    mine = self_copies()
    start(*mine)

    barrier = pltpu.get_barrier_semaphore()
    each(1, size, lambda step: pl.semaphore_signal(
        barrier, inc=1, device_id={"seq": (me + step) % size}, device_id_type=MESH))
    pl.semaphore_wait(barrier, size - 1)

    def far_device(step):
        return (cell * CELL + step // CELL * CELL + (spot + step) % CELL) % size

    def near_device(step):
        plane = (spot // HALF + step // HALF) % 2
        return cell * CELL + plane * HALF + (spot + step) % HALF

    def send_context(step):
        other = (chip + step) % chips

        @pl.when(other // KVH >= cell)
        def _():
            start(*context_copies(other))

    def send_far():
        each(CELL, size, lambda step: query_copy(far_device(step)).start())

    def send_far_context():
        each(KVH, chips, lambda step: send_context((cell * KVH + step - chip) % chips))

    def send_near_context():
        each(1, KVH, lambda step: send_context((cell * KVH + (head + step) % KVH - chip) % chips))

    def head_of(b, n):
        return qs[b, :, n * HD:(n + 1) * HD]

    def context_tile(t):
        at = pl.ds(t * (TILE // QBLK), TILE // QBLK)
        return ck[at].reshape(TILE, HD), cv[at].reshape(TILE, HD)

    def context_query(i):
        late = i // HALF
        q = [head_of(cell * CELL + i, n) for n in range(PAIR)]
        spots = i % HALF * rows + lax.broadcasted_iota(jnp.int32, (rows, TILE), 0)
        allowed = lax.broadcasted_iota(jnp.int32, (rows, TILE), 1) <= spots

        def causal(s):
            return jnp.where(allowed, s, NEG)

        def tile_steps(t, change):
            k, v = context_tile(t)
            return [(n, q[n], k, v, change) for n in range(PAIR)]

        def before(t, states):
            return run_steps(states, tile_steps(cell * SPAN + t, None))

        states = [(cm[i, n], cl[i, n], ca[i, n]) for n in range(PAIR)]
        states = run_steps(states, tile_steps(cell * SPAN + late, causal))
        return lax.fori_loop(0, late, before, states)

    def context_earlier(step):
        b = near_device(step)
        i = b % CELL

        @pl.when(step > 0)
        def _():
            query_arrival(b).wait_recv()

        q = [head_of(b, n) for n in range(PAIR)]

        def earlier(c, states):
            steps = []
            for t in range(SPAN):
                k, v = context_tile(c * SPAN + t)
                steps += [(n, q[n], k, v, None) for n in range(PAIR)]
            return run_steps(states, steps)

        for n, (m, l, acc) in enumerate(lax.fori_loop(0, cell, earlier, (fresh(rows),) * PAIR)):
            cm[i, n] = m
            cl[i, n] = l
            ca[i, n] = acc

    def pass_on(other):
        for copy in context_forwards(other * 2 + core):
            copy.wait_recv()
        start(*context_forwards(other * 2 + core))

    def arrive_context(other):
        for copy in context_forwards(other * 2 + 1 - core):
            copy.wait_recv()

    close = spot // HALF == inner
    each(1, size, lambda step: table_copy(step).start())

    each(1, KVH, lambda step: start(*store_copies((head + step) % KVH)))

    @pl.when(close)
    def _():
        send_far()

    each(1, HALF, lambda step: query_copy(near_device(step)).start())

    send_far_context()

    mine[4].wait()
    mine[5].wait()
    start(*store_forwards(spot))

    def drain_store(step):
        for copy in store_copies((head + step) % KVH):
            copy.wait_send()

    each(1, KVH, drain_store)

    @pl.when(jnp.logical_not(close))
    def _():
        send_far()

    @pl.when(close)
    def _():
        each(HALF, CELL, lambda step: query_copy(near_device(step)).start())
        send_near_context()

    mine[2].wait()
    mine[3].wait()
    start(*context_forwards(me))

    mine[1].wait()
    each(0, cell * KVH, lambda other: pass_on(other))
    each(0, cell * KVH, arrive_context)
    each(0, HALF, context_earlier)

    def relay_store(step):
        o = (head + step) % KVH * 2 + core
        for copy in store_forwards(o):
            copy.wait_recv()
        start(*store_forwards(o))

    each(1, KVH, relay_store)

    def arrive_store(other):
        for copy in store_forwards(other * 2 + 1 - core):
            copy.wait_recv()

    each(0, KVH, arrive_store)
    @pl.when(jnp.logical_not(close))
    def _():
        each(HALF, CELL, lambda step: query_copy(near_device(step)).start())
        send_near_context()

    mine[0].wait()
    each(1, size, lambda step: table_arrival(step).wait_recv())

    lane = lax.broadcasted_iota(jnp.int32, (rows, HD), 1)

    def memory_states(b):
        q = [head_of(b, n) for n in range(PAIR)]
        steps = []
        for t in range(PICKS // PER_TILE):
            ks, vs, gone = [], [], []
            for x in range(PER_TILE):
                pick = t * PER_TILE + x
                there = tb[b, pick % CAP * (HD // CAP) + cell * CELL + pick // CAP]
                at = pick // CAP * local + jnp.maximum(there, 0)
                ks.append(sk[at])
                vs.append(sv[at])
                gone.append(jnp.where(there < 0, NEG, 0.0).astype(jnp.float32))
            k, v = jnp.concatenate(ks, axis=0), jnp.concatenate(vs, axis=0)

            def hide(s, gone=gone):
                return jnp.concatenate(
                    [s[:, x * MROWS:(x + 1) * MROWS] + gone[x] for x in range(PER_TILE)], axis=1
                )

            steps += [(n, q[n], k, v, hide if masked else None) for n in range(PAIR)]
        return run_steps((None, None), steps)

    def serve_half(c, part):
        away = (cell + 1 + c) % cells
        first = ((cell - away + cells - 1) // cells + part) % 2 * HALF

        def serve(k, stats):
            b = away * CELL + first + k
            query_arrival(b).wait_recv()
            states = memory_states(b)
            slot = c * CELL + first + k
            for n in range(PAIR):
                m, l, acc = states[n]
                po[slot, :, n * HD:(n + 1) * HD] = (acc / l).astype(jnp.bfloat16)
                stats = jnp.where(lane == k * PAIR + n, m, stats)
                stats = jnp.where(lane == k * PAIR + n + STATS // 2, l, stats)
            partial_copy(slot).start()
            return stats

        stats = lax.fori_loop(0, HALF, serve, jnp.zeros((rows, HD), jnp.float32))
        ps[c * 2 + part] = stats.T[:STATS]
        stats_copy(c * 2 + part).start()

    def remember(step):
        b = near_device(step)
        i = b - cell * CELL

        for n, (m, l, acc) in enumerate(memory_states(b)):
            om[i, n] = m
            ol[i, n] = l
            oa[i, n] = acc

    for c in range(cells - 1):
        serve_half(c, 0)
    for c in range(cells - 1):
        serve_half(c, 1)
    each(0, HALF, remember)
    each(HALF, CELL, context_earlier)
    each(HALF, CELL, remember)

    each(1, KVH, lambda step: pass_on(cell * KVH + (head + step) % KVH))
    each(cell * KVH, (cell + 1) * KVH, arrive_context)

    def finish(k, part):
        i = (inner + part) % 2 * HALF + k
        near = context_query(i)
        for c in range(cells - 1):
            partial_copy(c * CELL + i).wait_recv()
        for n in range(PAIR):
            m, l, acc = om[i, n], ol[i, n], oa[i, n]
            for c in range(cells - 1):
                there = rt[c * 2 + part]
                m_far = jnp.sum(jnp.where(lane == k * PAIR + n, there, 0.0), axis=-1, keepdims=True)
                l_far = jnp.sum(jnp.where(lane == k * PAIR + n + STATS // 2, there, 0.0), axis=-1, keepdims=True)
                top = jnp.maximum(m, m_far)
                w = jnp.exp2((m - top) * SCALE2)
                w_far = jnp.exp2((m_far - top) * SCALE2) * l_far
                far = ro[c * CELL + i, :, n * HD:(n + 1) * HD].astype(jnp.float32)
                m, l, acc = top, l * w + w_far, acc * w + far * w_far
            memory = (acc / l).astype(jnp.bfloat16).astype(jnp.float32)
            context = (near[n][2] / near[n][1]).astype(jnp.bfloat16).astype(jnp.float32)
            gate = 1.0 / (1.0 + jnp.exp(-jnp.full((1, HD), gate_ref[spot * PAIR + n], jnp.float32)))
            os[i, :, n * HD:(n + 1) * HD] = (gate * memory + (1.0 - gate) * context).astype(jnp.bfloat16)

        @pl.when(i == spot)
        def _():
            result_self().start()

        @pl.when(i != spot)
        def _():
            result_copy(i).start()

    for part in range(2):
        for c in range(cells - 1):
            x = c * 2 + part
            stats_copy(x).wait_recv()
            rt[x] = jnp.concatenate([rs[x], jnp.zeros((HD - STATS, rows), jnp.float32)], axis=0).T
        each(0, HALF, lambda k, part=part: finish(k, part))

    result_self().wait()
    each(1, CELL, lambda step: result_arrival((spot + step) % CELL).wait_recv())
    each(1, CELL, lambda step: result_copy((spot + step) % CELL).wait_send())
    each(1, size, lambda step: table_copy(step).wait_send())
    each(1, size, lambda step: query_copy((me + step) % size).wait_send())

    def drain_context(step):
        other = (chip + step) % chips

        @pl.when(other // KVH >= cell)
        def _():
            for copy in context_copies(other):
                copy.wait_send()

    each(1, chips, drain_context)

    def drain_forward(other):
        for copy in context_forwards(other * 2 + core):
            copy.wait_send()

    each(0, (cell + 1) * KVH, drain_forward)

    def drain_store_forward(other):
        for copy in store_forwards(other * 2 + core):
            copy.wait_send()

    each(0, KVH, drain_store_forward)
    each(0, (cells - 1) * CELL, lambda slot: partial_copy(slot).wait_send())
    each(0, 2 * (cells - 1), lambda x: stats_copy(x).wait_send())


def attention_call(gate, table, queries, keys, values, store_keys, store_values, size):
    rows = queries.shape[0]
    cells = size // CELL
    chips = size // 2
    local = store_keys.shape[0]
    far = max(cells - 1, 1)
    block = (rows, WIDTH)
    dma = pltpu.SemaphoreType.DMA
    return pl.pallas_call(
        functools.partial(attention_kernel, size, size * CAP != TOPM),
        out_shape=jax.ShapeDtypeStruct(queries.shape, jnp.bfloat16),
        in_specs=[pl.BlockSpec(memory_space=pltpu.SMEM)] + [pl.BlockSpec(memory_space=pl.ANY)] * 6,
        out_specs=pl.BlockSpec(memory_space=pltpu.VMEM),
        scratch_shapes=[
            pltpu.SMEM((size, HD), jnp.int32),
            pltpu.VMEM((size, *block), jnp.bfloat16),
            pltpu.VMEM((size, rows, HD), jnp.bfloat16),
            pltpu.VMEM((size, rows, HD), jnp.bfloat16),
            pltpu.VMEM((CELL * local, MROWS, HD), jnp.bfloat16),
            pltpu.VMEM((CELL * local, MROWS, HD), jnp.bfloat16),
            pltpu.VMEM((CELL, PAIR, rows, 1), jnp.float32),
            pltpu.VMEM((CELL, PAIR, rows, 1), jnp.float32),
            pltpu.VMEM((CELL, PAIR, rows, HD), jnp.float32),
            pltpu.VMEM((CELL, PAIR, rows, 1), jnp.float32),
            pltpu.VMEM((CELL, PAIR, rows, 1), jnp.float32),
            pltpu.VMEM((CELL, PAIR, rows, HD), jnp.float32),
            pltpu.VMEM((far * CELL, *block), jnp.bfloat16),
            pltpu.VMEM((far * CELL, *block), jnp.bfloat16),
            pltpu.VMEM((2 * far, STATS, rows), jnp.float32),
            pltpu.VMEM((2 * far, STATS, rows), jnp.float32),
            pltpu.VMEM((2 * far, rows, HD), jnp.float32),
            pltpu.VMEM((CELL, *block), jnp.bfloat16),
            dma((2, size)),
            dma((2, size)),
            dma((2, chips)),
            dma((2, size)),
            dma((2, chips)),
            dma((2, KVH)),
            dma((2, CELL)),
            dma((2, KVH)),
            dma((2, far * CELL)),
            dma((2, 2 * far)),
            dma((2, CELL)),
            dma((7,)),
        ],
        compiler_params=pltpu.CompilerParams(
            collective_id=0, has_side_effects=True, vmem_limit_bytes=VMEM_LIMIT
        ),
        cost_estimate=pl.CostEstimate(
            flops=16 * 4096 * 256 * 512, bytes_accessed=20_000_000, transcendentals=16 * 4096 * 256
        ),
    )(gate, table, queries, keys, values, store_keys, store_values)


def on_device(
    queries, ctx_keys, ctx_values, store_keys, store_values, block_ids, block_slot, gate_logit
):
    size = lax.axis_size("seq")
    local_count = store_keys.shape[0]
    my_slots = lookup_slots(block_ids.reshape(-1), block_slot)
    table = request_table(my_slots, HD // CAP, local_count)
    return attention_call(gate_logit, table, queries, ctx_keys, ctx_values, store_keys, store_values, size)


def solution(mesh):
    placed = (
        P(("groups", "seq"), None),
        P(("groups", "seq"), None),
        P(("groups", "seq"), None),
        P(("groups", "seq"), None, None),
        P(("groups", "seq"), None, None),
        P(("groups", "seq"), None),
        P("groups"),
        P(),
    )
    return jax.shard_map(
        on_device, mesh=mesh, in_specs=placed, out_specs=P(("groups", "seq"), None), check_vma=False
    )
```

```python
import functools

import jax
import jax.numpy as jnp
from jax import lax
from jax.experimental import pallas as pl
from jax.experimental.pallas import tpu as pltpu
from jax.sharding import PartitionSpec as P

H = 16
KVH = 4
HD = 128
GROUP = H // KVH
QBLK = 256
MROWS = 128
TOPM = 32
CAP = 2
CELL = 2 * KVH
PAIR = 2
WIDTH = PAIR * HD
TILE = 1024
SPAN = CELL * QBLK // TILE
PICKS = CELL * CAP
PER_TILE = TILE // MROWS
HALF = CELL // 2
STATS = 2 * HALF * PAIR

NEG = -1e30
SCALE2 = HD ** (-0.5) * 1.4426950408889634
VMEM_LIMIT = 60 * 1024 * 1024
MESH = pl.DeviceIdType.MESH


def request_table(slots, owners_count, local_count):
    owner = slots // local_count
    local = slots % local_count
    held = owner[None, :] == jnp.arange(owners_count, dtype=jnp.int32)[:, None]
    high = jnp.max(jnp.where(held, local[None, :], -1), axis=1)
    low = jnp.min(jnp.where(held, local[None, :], local_count), axis=1)
    return jnp.concatenate([high, jnp.where(low < high, low, -1)])


def lookup_slots(wanted_ids, block_slot):
    hits = wanted_ids[..., None] == jnp.arange(block_slot.shape[0], dtype=jnp.int32)
    return jnp.sum(jnp.where(hits, block_slot, 0), axis=-1)


def fresh(rows):
    return (
        jnp.full((rows, 1), NEG, jnp.float32),
        jnp.zeros((rows, 1), jnp.float32),
        jnp.zeros((rows, HD), jnp.float32),
    )


def scores(q, k):
    return lax.dot_general(q, k, (((1,), (1,)), ((), ())), preferred_element_type=jnp.float32)


def absorb(state, s, v):
    if state is None:
        m = jnp.max(s, axis=-1, keepdims=True)
        p = jnp.exp2((s - m) * SCALE2)
        l = jnp.sum(p, axis=-1, keepdims=True)
        return m, l, jnp.dot(p.astype(jnp.bfloat16), v, preferred_element_type=jnp.float32)
    m, l, acc = state
    m_new = jnp.maximum(m, jnp.max(s, axis=-1, keepdims=True))
    decay = jnp.exp2((m - m_new) * SCALE2)
    p = jnp.exp2((s - m_new) * SCALE2)
    l = l * decay + jnp.sum(p, axis=-1, keepdims=True)
    acc = acc * decay + jnp.dot(p.astype(jnp.bfloat16), v, preferred_element_type=jnp.float32)
    return m_new, l, acc


def run_steps(states, steps):
    states = list(states)
    ahead = scores(*steps[0][1:3])
    for n, (head, _, _, v, change) in enumerate(steps):
        s = ahead
        if n + 1 < len(steps):
            ahead = scores(*steps[n + 1][1:3])
        if change is not None:
            s = change(s)
        states[head] = absorb(states[head], s, v)
    return tuple(states)


def attention_kernel(size, masked, gate_ref, table_ref, q_ref, key_ref, value_ref, sk_ref, sv_ref, out_ref,
                     tb, qs, ck, cv, sk, sv, om, ol, oa, cm, cl, ca, po, ro, ps, rs, rt, os,
                     t_sem, q_sem, kv_send, kv_recv, kv_fwd, st_send, st_recv, st_fwd,
                     po_sem, ps_sem, out_sem, self_sem):
    cells = size // CELL
    chips = size // 2
    me = lax.axis_index("seq")
    cell = me // CELL
    spot = me % CELL
    chip = me // 2
    head = chip % KVH
    core = me % 2
    peer = chip * 2 + 1 - core
    inner = 1 - 2 * cell // cells
    rows = q_ref.shape[0]
    local = sk_ref.shape[0]

    def lanes_of(j, width):
        return pl.ds(pl.multiple_of(j * width, width), width)

    def remote(src, dst, send, recv, device):
        return pltpu.make_async_remote_copy(
            src_ref=src, dst_ref=dst, send_sem=send, recv_sem=recv,
            device_id={"seq": device}, device_id_type=MESH,
        )

    def table_copy(step):
        return remote(table_ref, tb.at[me], t_sem.at[0, step], t_sem.at[1, me], (me + step) % size)

    def table_arrival(step):
        return remote(table_ref, tb.at[(me + step) % size], t_sem.at[0, step], t_sem.at[1, (me + step) % size], peer)

    def query_copy(device):
        return remote(q_ref.at[:, lanes_of(device % CELL, WIDTH)], qs.at[me],
                      q_sem.at[0, device], q_sem.at[1, me], device)

    def query_arrival(device):
        return remote(qs.at[device], qs.at[device], q_sem.at[0, device], q_sem.at[1, device], peer)

    def context_copies(other):
        return tuple(
            remote(src.at[:, lanes_of(other % KVH, HD)], dst.at[me],
                   kv_send.at[w, other], kv_recv.at[w, me], other * 2 + core)
            for w, (src, dst) in enumerate(((key_ref, ck), (value_ref, cv)))
        )

    def context_forwards(source):
        return tuple(
            remote(buf.at[source], buf.at[source], kv_fwd.at[w, source // 2], kv_recv.at[w, source], peer)
            for w, buf in enumerate((ck, cv))
        )

    def owned(o):
        return pl.ds(pl.multiple_of(o * local, local), local)

    def store_copies(other):
        return tuple(
            remote(src.at[:, :, lanes_of(other, HD)], dst.at[owned(spot)],
                   st_send.at[w, other], st_recv.at[w, spot], cell * CELL + other * 2 + core)
            for w, (src, dst) in enumerate(((sk_ref, sk), (sv_ref, sv)))
        )

    def store_forwards(o):
        return tuple(
            remote(buf.at[owned(o)], buf.at[owned(o)], st_fwd.at[w, o // 2], st_recv.at[w, o], peer)
            for w, buf in enumerate((sk, sv))
        )

    def self_copies():
        return (
            pltpu.make_async_copy(table_ref, tb.at[me], self_sem.at[0]),
            pltpu.make_async_copy(q_ref.at[:, lanes_of(spot, WIDTH)], qs.at[me], self_sem.at[1]),
            pltpu.make_async_copy(key_ref.at[:, lanes_of(head, HD)], ck.at[me], self_sem.at[2]),
            pltpu.make_async_copy(value_ref.at[:, lanes_of(head, HD)], cv.at[me], self_sem.at[3]),
            pltpu.make_async_copy(sk_ref.at[:, :, lanes_of(head, HD)], sk.at[owned(spot)], self_sem.at[4]),
            pltpu.make_async_copy(sv_ref.at[:, :, lanes_of(head, HD)], sv.at[owned(spot)], self_sem.at[5]),
        )

    def partial_copy(slot):
        away = (cell + 1 + slot // CELL) % cells
        return remote(po.at[slot], ro.at[slot], po_sem.at[0, slot], po_sem.at[1, slot], away * CELL + spot)

    def stats_copy(x):
        return remote(ps.at[x], rs.at[x], ps_sem.at[0, x], ps_sem.at[1, x], (cell + 1 + x // 2) % cells * CELL + spot)

    def result_copy(i):
        return remote(os.at[i], out_ref.at[:, lanes_of(spot, WIDTH)],
                      out_sem.at[0, i], out_sem.at[1, spot], cell * CELL + i)

    def result_arrival(u):
        return remote(os.at[0], out_ref.at[:, lanes_of(u, WIDTH)], out_sem.at[0, u], out_sem.at[1, u], peer)

    def result_self():
        return pltpu.make_async_copy(os.at[spot], out_ref.at[:, lanes_of(spot, WIDTH)], self_sem.at[6])

    def each(low, high, body):
        def step(i, carry):
            body(i)
            return carry

        lax.fori_loop(low, high, step, 0)

    def start(*copies):
        for copy in copies:
            copy.start()

    mine = self_copies()
    start(*mine)

    barrier = pltpu.get_barrier_semaphore()
    each(1, size, lambda step: pl.semaphore_signal(
        barrier, inc=1, device_id={"seq": (me + step) % size}, device_id_type=MESH))
    pl.semaphore_wait(barrier, size - 1)

    def far_device(step):
        return (cell * CELL + step // CELL * CELL + (spot + step) % CELL) % size

    def near_device(step):
        plane = (spot // HALF + step // HALF) % 2
        return cell * CELL + plane * HALF + (spot + step) % HALF

    def send_context(step):
        other = (chip + step) % chips

        @pl.when(other // KVH >= cell)
        def _():
            start(*context_copies(other))

    def send_far():
        each(CELL, size, lambda step: query_copy(far_device(step)).start())

    def send_far_context():
        each(KVH, chips, lambda step: send_context((cell * KVH + step - chip) % chips))

    def send_near_context():
        each(1, KVH, lambda step: send_context((cell * KVH + (head + step) % KVH - chip) % chips))

    def head_of(b, n):
        return qs[b, :, n * HD:(n + 1) * HD]

    def context_tile(t):
        at = pl.ds(t * (TILE // QBLK), TILE // QBLK)
        return ck[at].reshape(TILE, HD), cv[at].reshape(TILE, HD)

    def context_query(i):
        late = i // HALF
        q = [head_of(cell * CELL + i, n) for n in range(PAIR)]
        spots = i % HALF * rows + lax.broadcasted_iota(jnp.int32, (rows, TILE), 0)
        allowed = lax.broadcasted_iota(jnp.int32, (rows, TILE), 1) <= spots

        def causal(s):
            return jnp.where(allowed, s, NEG)

        def tile_steps(t, change):
            k, v = context_tile(t)
            return [(n, q[n], k, v, change) for n in range(PAIR)]

        def before(t, states):
            return run_steps(states, tile_steps(cell * SPAN + t, None))

        states = [(cm[i, n], cl[i, n], ca[i, n]) for n in range(PAIR)]
        states = run_steps(states, tile_steps(cell * SPAN + late, causal))
        return lax.fori_loop(0, late, before, states)

    def context_earlier(step):
        b = near_device(step)
        i = b % CELL

        @pl.when(step > 0)
        def _():
            query_arrival(b).wait_recv()

        q = [head_of(b, n) for n in range(PAIR)]

        def earlier(c, states):
            steps = []
            for t in range(SPAN):
                k, v = context_tile(c * SPAN + t)
                steps += [(n, q[n], k, v, None) for n in range(PAIR)]
            return run_steps(states, steps)

        for n, (m, l, acc) in enumerate(lax.fori_loop(0, cell, earlier, (fresh(rows),) * PAIR)):
            cm[i, n] = m
            cl[i, n] = l
            ca[i, n] = acc

    def pass_on(other):
        for copy in context_forwards(other * 2 + core):
            copy.wait_recv()
        start(*context_forwards(other * 2 + core))

    def arrive_context(other):
        for copy in context_forwards(other * 2 + 1 - core):
            copy.wait_recv()

    close = spot // HALF == inner
    each(1, size, lambda step: table_copy(step).start())

    each(1, KVH, lambda step: start(*store_copies((head + step) % KVH)))

    @pl.when(close)
    def _():
        send_far()

    each(1, HALF, lambda step: query_copy(near_device(step)).start())

    send_far_context()

    mine[4].wait()
    mine[5].wait()
    start(*store_forwards(spot))

    def drain_store(step):
        for copy in store_copies((head + step) % KVH):
            copy.wait_send()

    each(1, KVH, drain_store)

    @pl.when(jnp.logical_not(close))
    def _():
        send_far()

    @pl.when(close)
    def _():
        each(HALF, CELL, lambda step: query_copy(near_device(step)).start())
        send_near_context()

    mine[2].wait()
    mine[3].wait()
    start(*context_forwards(me))

    mine[1].wait()
    each(0, cell * KVH, lambda other: pass_on(other))
    each(0, cell * KVH, arrive_context)
    each(0, HALF, context_earlier)

    def relay_store(step):
        o = (head + step) % KVH * 2 + core
        for copy in store_forwards(o):
            copy.wait_recv()
        start(*store_forwards(o))

    each(1, KVH, relay_store)

    def arrive_store(other):
        for copy in store_forwards(other * 2 + 1 - core):
            copy.wait_recv()

    each(0, KVH, arrive_store)
    mine[0].wait()
    each(1, size, lambda step: table_arrival(step).wait_recv())

    lane = lax.broadcasted_iota(jnp.int32, (rows, HD), 1)

    def memory_states(b):
        q = [head_of(b, n) for n in range(PAIR)]
        steps = []
        for t in range(PICKS // PER_TILE):
            ks, vs, gone = [], [], []
            for x in range(PER_TILE):
                pick = t * PER_TILE + x
                there = tb[b, pick % CAP * (HD // CAP) + cell * CELL + pick // CAP]
                at = pick // CAP * local + jnp.maximum(there, 0)
                ks.append(sk[at])
                vs.append(sv[at])
                gone.append(jnp.where(there < 0, NEG, 0.0).astype(jnp.float32))
            k, v = jnp.concatenate(ks, axis=0), jnp.concatenate(vs, axis=0)

            def hide(s, gone=gone):
                return jnp.concatenate(
                    [s[:, x * MROWS:(x + 1) * MROWS] + gone[x] for x in range(PER_TILE)], axis=1
                )

            steps += [(n, q[n], k, v, hide if masked else None) for n in range(PAIR)]
        return run_steps((None, None), steps)

    def serve_half(c, part):
        away = (cell + 1 + c) % cells
        first = ((cell - away + cells - 1) // cells + part) % 2 * HALF

        def serve(k, stats):
            b = away * CELL + first + k
            query_arrival(b).wait_recv()
            states = memory_states(b)
            slot = c * CELL + first + k
            for n in range(PAIR):
                m, l, acc = states[n]
                po[slot, :, n * HD:(n + 1) * HD] = (acc / l).astype(jnp.bfloat16)
                stats = jnp.where(lane == k * PAIR + n, m, stats)
                stats = jnp.where(lane == k * PAIR + n + STATS // 2, l, stats)
            partial_copy(slot).start()
            return stats

        stats = lax.fori_loop(0, HALF, serve, jnp.zeros((rows, HD), jnp.float32))
        ps[c * 2 + part] = stats.T[:STATS]
        stats_copy(c * 2 + part).start()

    def remember(step):
        b = near_device(step)
        i = b - cell * CELL

        for n, (m, l, acc) in enumerate(memory_states(b)):
            om[i, n] = m
            ol[i, n] = l
            oa[i, n] = acc

    for c in range(cells - 1):
        serve_half(c, 0)
    @pl.when(jnp.logical_not(close))
    def _():
        each(HALF, CELL, lambda step: query_copy(near_device(step)).start())
        send_near_context()

    for c in range(cells - 1):
        serve_half(c, 1)
    each(0, HALF, remember)
    each(HALF, CELL, context_earlier)
    each(HALF, CELL, remember)

    each(1, KVH, lambda step: pass_on(cell * KVH + (head + step) % KVH))
    each(cell * KVH, (cell + 1) * KVH, arrive_context)

    def finish(k, part):
        i = (inner + part) % 2 * HALF + k
        near = context_query(i)
        for c in range(cells - 1):
            partial_copy(c * CELL + i).wait_recv()
        for n in range(PAIR):
            m, l, acc = om[i, n], ol[i, n], oa[i, n]
            for c in range(cells - 1):
                there = rt[c * 2 + part]
                m_far = jnp.sum(jnp.where(lane == k * PAIR + n, there, 0.0), axis=-1, keepdims=True)
                l_far = jnp.sum(jnp.where(lane == k * PAIR + n + STATS // 2, there, 0.0), axis=-1, keepdims=True)
                top = jnp.maximum(m, m_far)
                w = jnp.exp2((m - top) * SCALE2)
                w_far = jnp.exp2((m_far - top) * SCALE2) * l_far
                far = ro[c * CELL + i, :, n * HD:(n + 1) * HD].astype(jnp.float32)
                m, l, acc = top, l * w + w_far, acc * w + far * w_far
            memory = (acc / l).astype(jnp.bfloat16).astype(jnp.float32)
            context = (near[n][2] / near[n][1]).astype(jnp.bfloat16).astype(jnp.float32)
            gate = 1.0 / (1.0 + jnp.exp(-jnp.full((1, HD), gate_ref[spot * PAIR + n], jnp.float32)))
            os[i, :, n * HD:(n + 1) * HD] = (gate * memory + (1.0 - gate) * context).astype(jnp.bfloat16)

        @pl.when(i == spot)
        def _():
            result_self().start()

        @pl.when(i != spot)
        def _():
            result_copy(i).start()

    for part in range(2):
        for c in range(cells - 1):
            x = c * 2 + part
            stats_copy(x).wait_recv()
            rt[x] = jnp.concatenate([rs[x], jnp.zeros((HD - STATS, rows), jnp.float32)], axis=0).T
        each(0, HALF, lambda k, part=part: finish(k, part))

    result_self().wait()
    each(1, CELL, lambda step: result_arrival((spot + step) % CELL).wait_recv())
    each(1, CELL, lambda step: result_copy((spot + step) % CELL).wait_send())
    each(1, size, lambda step: table_copy(step).wait_send())
    each(1, size, lambda step: query_copy((me + step) % size).wait_send())

    def drain_context(step):
        other = (chip + step) % chips

        @pl.when(other // KVH >= cell)
        def _():
            for copy in context_copies(other):
                copy.wait_send()

    each(1, chips, drain_context)

    def drain_forward(other):
        for copy in context_forwards(other * 2 + core):
            copy.wait_send()

    each(0, (cell + 1) * KVH, drain_forward)

    def drain_store_forward(other):
        for copy in store_forwards(other * 2 + core):
            copy.wait_send()

    each(0, KVH, drain_store_forward)
    each(0, (cells - 1) * CELL, lambda slot: partial_copy(slot).wait_send())
    each(0, 2 * (cells - 1), lambda x: stats_copy(x).wait_send())


def attention_call(gate, table, queries, keys, values, store_keys, store_values, size):
    rows = queries.shape[0]
    cells = size // CELL
    chips = size // 2
    local = store_keys.shape[0]
    far = max(cells - 1, 1)
    block = (rows, WIDTH)
    dma = pltpu.SemaphoreType.DMA
    return pl.pallas_call(
        functools.partial(attention_kernel, size, size * CAP != TOPM),
        out_shape=jax.ShapeDtypeStruct(queries.shape, jnp.bfloat16),
        in_specs=[pl.BlockSpec(memory_space=pltpu.SMEM)] + [pl.BlockSpec(memory_space=pl.ANY)] * 6,
        out_specs=pl.BlockSpec(memory_space=pltpu.VMEM),
        scratch_shapes=[
            pltpu.SMEM((size, HD), jnp.int32),
            pltpu.VMEM((size, *block), jnp.bfloat16),
            pltpu.VMEM((size, rows, HD), jnp.bfloat16),
            pltpu.VMEM((size, rows, HD), jnp.bfloat16),
            pltpu.VMEM((CELL * local, MROWS, HD), jnp.bfloat16),
            pltpu.VMEM((CELL * local, MROWS, HD), jnp.bfloat16),
            pltpu.VMEM((CELL, PAIR, rows, 1), jnp.float32),
            pltpu.VMEM((CELL, PAIR, rows, 1), jnp.float32),
            pltpu.VMEM((CELL, PAIR, rows, HD), jnp.float32),
            pltpu.VMEM((CELL, PAIR, rows, 1), jnp.float32),
            pltpu.VMEM((CELL, PAIR, rows, 1), jnp.float32),
            pltpu.VMEM((CELL, PAIR, rows, HD), jnp.float32),
            pltpu.VMEM((far * CELL, *block), jnp.bfloat16),
            pltpu.VMEM((far * CELL, *block), jnp.bfloat16),
            pltpu.VMEM((2 * far, STATS, rows), jnp.float32),
            pltpu.VMEM((2 * far, STATS, rows), jnp.float32),
            pltpu.VMEM((2 * far, rows, HD), jnp.float32),
            pltpu.VMEM((CELL, *block), jnp.bfloat16),
            dma((2, size)),
            dma((2, size)),
            dma((2, chips)),
            dma((2, size)),
            dma((2, chips)),
            dma((2, KVH)),
            dma((2, CELL)),
            dma((2, KVH)),
            dma((2, far * CELL)),
            dma((2, 2 * far)),
            dma((2, CELL)),
            dma((7,)),
        ],
        compiler_params=pltpu.CompilerParams(
            collective_id=0, has_side_effects=True, vmem_limit_bytes=VMEM_LIMIT
        ),
        cost_estimate=pl.CostEstimate(
            flops=16 * 4096 * 256 * 512, bytes_accessed=20_000_000, transcendentals=16 * 4096 * 256
        ),
    )(gate, table, queries, keys, values, store_keys, store_values)


def on_device(
    queries, ctx_keys, ctx_values, store_keys, store_values, block_ids, block_slot, gate_logit
):
    size = lax.axis_size("seq")
    local_count = store_keys.shape[0]
    my_slots = lookup_slots(block_ids.reshape(-1), block_slot)
    table = request_table(my_slots, HD // CAP, local_count)
    return attention_call(gate_logit, table, queries, ctx_keys, ctx_values, store_keys, store_values, size)


def solution(mesh):
    placed = (
        P(("groups", "seq"), None),
        P(("groups", "seq"), None),
        P(("groups", "seq"), None),
        P(("groups", "seq"), None, None),
        P(("groups", "seq"), None, None),
        P(("groups", "seq"), None),
        P("groups"),
        P(),
    )
    return jax.shard_map(
        on_device, mesh=mesh, in_specs=placed, out_specs=P(("groups", "seq"), None), check_vma=False
    )
```

```python
import functools

import jax
import jax.numpy as jnp
from jax import lax
from jax.experimental import pallas as pl
from jax.experimental.pallas import tpu as pltpu
from jax.sharding import PartitionSpec as P

H = 16
KVH = 4
HD = 128
GROUP = H // KVH
QBLK = 256
MROWS = 128
TOPM = 32
CAP = 2
CELL = 2 * KVH
PAIR = 2
WIDTH = PAIR * HD
TILE = 1024
SPAN = CELL * QBLK // TILE
PICKS = CELL * CAP
PER_TILE = TILE // MROWS
HALF = CELL // 2
STATS = 2 * HALF * PAIR

NEG = -1e30
SCALE2 = HD ** (-0.5) * 1.4426950408889634
VMEM_LIMIT = 60 * 1024 * 1024
MESH = pl.DeviceIdType.MESH


def request_table(slots, owners_count, local_count):
    owner = slots // local_count
    local = slots % local_count
    held = owner[None, :] == jnp.arange(owners_count, dtype=jnp.int32)[:, None]
    high = jnp.max(jnp.where(held, local[None, :], -1), axis=1)
    low = jnp.min(jnp.where(held, local[None, :], local_count), axis=1)
    return jnp.concatenate([high, jnp.where(low < high, low, -1)])


def lookup_slots(wanted_ids, block_slot):
    hits = wanted_ids[..., None] == jnp.arange(block_slot.shape[0], dtype=jnp.int32)
    return jnp.sum(jnp.where(hits, block_slot, 0), axis=-1)


def fresh(rows):
    return (
        jnp.full((rows, 1), NEG, jnp.float32),
        jnp.zeros((rows, 1), jnp.float32),
        jnp.zeros((rows, HD), jnp.float32),
    )


def scores(q, k):
    return lax.dot_general(q, k, (((1,), (1,)), ((), ())), preferred_element_type=jnp.float32)


def absorb(state, s, v):
    if state is None:
        m = jnp.max(s, axis=-1, keepdims=True)
        p = jnp.exp2((s - m) * SCALE2)
        l = jnp.sum(p, axis=-1, keepdims=True)
        return m, l, jnp.dot(p.astype(jnp.bfloat16), v, preferred_element_type=jnp.float32)
    m, l, acc = state
    m_new = jnp.maximum(m, jnp.max(s, axis=-1, keepdims=True))
    decay = jnp.exp2((m - m_new) * SCALE2)
    p = jnp.exp2((s - m_new) * SCALE2)
    l = l * decay + jnp.sum(p, axis=-1, keepdims=True)
    acc = acc * decay + jnp.dot(p.astype(jnp.bfloat16), v, preferred_element_type=jnp.float32)
    return m_new, l, acc


def run_steps(states, steps):
    states = list(states)
    ahead = scores(*steps[0][1:3])
    for n, (head, _, _, v, change) in enumerate(steps):
        s = ahead
        if n + 1 < len(steps):
            ahead = scores(*steps[n + 1][1:3])
        if change is not None:
            s = change(s)
        states[head] = absorb(states[head], s, v)
    return tuple(states)


def attention_kernel(size, masked, gate_ref, table_ref, q_ref, key_ref, value_ref, sk_ref, sv_ref, out_ref,
                     tb, qs, ck, cv, sk, sv, om, ol, oa, cm, cl, ca, po, ro, ps, rs, rt, os,
                     t_sem, q_sem, kv_send, kv_recv, kv_fwd, st_send, st_recv, st_fwd,
                     po_sem, ps_sem, out_sem, self_sem):
    cells = size // CELL
    chips = size // 2
    me = lax.axis_index("seq")
    cell = me // CELL
    spot = me % CELL
    chip = me // 2
    head = chip % KVH
    core = me % 2
    peer = chip * 2 + 1 - core
    inner = 1 - 2 * cell // cells
    rows = q_ref.shape[0]
    local = sk_ref.shape[0]

    def lanes_of(j, width):
        return pl.ds(pl.multiple_of(j * width, width), width)

    def remote(src, dst, send, recv, device):
        return pltpu.make_async_remote_copy(
            src_ref=src, dst_ref=dst, send_sem=send, recv_sem=recv,
            device_id={"seq": device}, device_id_type=MESH,
        )

    def table_copy(step):
        return remote(table_ref, tb.at[me], t_sem.at[0, step], t_sem.at[1, me], (me + step) % size)

    def table_arrival(step):
        return remote(table_ref, tb.at[(me + step) % size], t_sem.at[0, step], t_sem.at[1, (me + step) % size], peer)

    def query_copy(device):
        return remote(q_ref.at[:, lanes_of(device % CELL, WIDTH)], qs.at[me],
                      q_sem.at[0, device], q_sem.at[1, me], device)

    def query_arrival(device):
        return remote(qs.at[device], qs.at[device], q_sem.at[0, device], q_sem.at[1, device], peer)

    def context_copies(other):
        return tuple(
            remote(src.at[:, lanes_of(other % KVH, HD)], dst.at[me],
                   kv_send.at[w, other], kv_recv.at[w, me], other * 2 + core)
            for w, (src, dst) in enumerate(((key_ref, ck), (value_ref, cv)))
        )

    def context_forwards(source):
        return tuple(
            remote(buf.at[source], buf.at[source], kv_fwd.at[w, source // 2], kv_recv.at[w, source], peer)
            for w, buf in enumerate((ck, cv))
        )

    def owned(o):
        return pl.ds(pl.multiple_of(o * local, local), local)

    def store_copies(other):
        return tuple(
            remote(src.at[:, :, lanes_of(other, HD)], dst.at[owned(spot)],
                   st_send.at[w, other], st_recv.at[w, spot], cell * CELL + other * 2 + core)
            for w, (src, dst) in enumerate(((sk_ref, sk), (sv_ref, sv)))
        )

    def store_forwards(o):
        return tuple(
            remote(buf.at[owned(o)], buf.at[owned(o)], st_fwd.at[w, o // 2], st_recv.at[w, o], peer)
            for w, buf in enumerate((sk, sv))
        )

    def self_copies():
        return (
            pltpu.make_async_copy(table_ref, tb.at[me], self_sem.at[0]),
            pltpu.make_async_copy(q_ref.at[:, lanes_of(spot, WIDTH)], qs.at[me], self_sem.at[1]),
            pltpu.make_async_copy(key_ref.at[:, lanes_of(head, HD)], ck.at[me], self_sem.at[2]),
            pltpu.make_async_copy(value_ref.at[:, lanes_of(head, HD)], cv.at[me], self_sem.at[3]),
            pltpu.make_async_copy(sk_ref.at[:, :, lanes_of(head, HD)], sk.at[owned(spot)], self_sem.at[4]),
            pltpu.make_async_copy(sv_ref.at[:, :, lanes_of(head, HD)], sv.at[owned(spot)], self_sem.at[5]),
        )

    def partial_copy(slot):
        away = (cell + 1 + slot // CELL) % cells
        return remote(po.at[slot], ro.at[slot], po_sem.at[0, slot], po_sem.at[1, slot], away * CELL + spot)

    def stats_copy(x):
        return remote(ps.at[x], rs.at[x], ps_sem.at[0, x], ps_sem.at[1, x], (cell + 1 + x // 2) % cells * CELL + spot)

    def result_copy(i):
        return remote(os.at[i], out_ref.at[:, lanes_of(spot, WIDTH)],
                      out_sem.at[0, i], out_sem.at[1, spot], cell * CELL + i)

    def result_arrival(u):
        return remote(os.at[0], out_ref.at[:, lanes_of(u, WIDTH)], out_sem.at[0, u], out_sem.at[1, u], peer)

    def result_self():
        return pltpu.make_async_copy(os.at[spot], out_ref.at[:, lanes_of(spot, WIDTH)], self_sem.at[6])

    def each(low, high, body):
        def step(i, carry):
            body(i)
            return carry

        lax.fori_loop(low, high, step, 0)

    def start(*copies):
        for copy in copies:
            copy.start()

    barrier = pltpu.get_barrier_semaphore()
    each(1, size, lambda step: pl.semaphore_signal(
        barrier, inc=1, device_id={"seq": (me + step) % size}, device_id_type=MESH))
    mine = self_copies()
    start(*mine)
    pl.semaphore_wait(barrier, size - 1)

    def far_device(step):
        return (cell * CELL + step // CELL * CELL + (spot + step) % CELL) % size

    def near_device(step):
        plane = (spot // HALF + step // HALF) % 2
        return cell * CELL + plane * HALF + (spot + step) % HALF

    def send_context(step):
        other = (chip + step) % chips

        @pl.when(other // KVH >= cell)
        def _():
            start(*context_copies(other))

    def send_far():
        each(CELL, size, lambda step: query_copy(far_device(step)).start())

    def send_far_context():
        each(KVH, chips, lambda step: send_context((cell * KVH + step - chip) % chips))

    def send_near_context():
        each(1, KVH, lambda step: send_context((cell * KVH + (head + step) % KVH - chip) % chips))

    def head_of(b, n):
        return qs[b, :, n * HD:(n + 1) * HD]

    def context_tile(t):
        at = pl.ds(t * (TILE // QBLK), TILE // QBLK)
        return ck[at].reshape(TILE, HD), cv[at].reshape(TILE, HD)

    def context_query(i):
        late = i // HALF
        q = [head_of(cell * CELL + i, n) for n in range(PAIR)]
        spots = i % HALF * rows + lax.broadcasted_iota(jnp.int32, (rows, TILE), 0)
        allowed = lax.broadcasted_iota(jnp.int32, (rows, TILE), 1) <= spots

        def causal(s):
            return jnp.where(allowed, s, NEG)

        def tile_steps(t, change):
            k, v = context_tile(t)
            return [(n, q[n], k, v, change) for n in range(PAIR)]

        def before(t, states):
            return run_steps(states, tile_steps(cell * SPAN + t, None))

        states = [(cm[i, n], cl[i, n], ca[i, n]) for n in range(PAIR)]
        states = run_steps(states, tile_steps(cell * SPAN + late, causal))
        return lax.fori_loop(0, late, before, states)

    def context_earlier(step):
        b = near_device(step)
        i = b % CELL

        @pl.when(step > 0)
        def _():
            query_arrival(b).wait_recv()

        q = [head_of(b, n) for n in range(PAIR)]

        def earlier(c, states):
            steps = []
            for t in range(SPAN):
                k, v = context_tile(c * SPAN + t)
                steps += [(n, q[n], k, v, None) for n in range(PAIR)]
            return run_steps(states, steps)

        for n, (m, l, acc) in enumerate(lax.fori_loop(0, cell, earlier, (fresh(rows),) * PAIR)):
            cm[i, n] = m
            cl[i, n] = l
            ca[i, n] = acc

    def pass_on(other):
        for copy in context_forwards(other * 2 + core):
            copy.wait_recv()
        start(*context_forwards(other * 2 + core))

    def arrive_context(other):
        for copy in context_forwards(other * 2 + 1 - core):
            copy.wait_recv()

    close = spot // HALF == inner
    each(1, size, lambda step: table_copy(step).start())

    each(1, KVH, lambda step: start(*store_copies((head + step) % KVH)))

    @pl.when(close)
    def _():
        send_far()

    each(1, HALF, lambda step: query_copy(near_device(step)).start())

    send_far_context()

    mine[4].wait()
    mine[5].wait()
    start(*store_forwards(spot))

    def drain_store(step):
        for copy in store_copies((head + step) % KVH):
            copy.wait_send()

    each(1, KVH, drain_store)

    @pl.when(jnp.logical_not(close))
    def _():
        send_far()

    @pl.when(close)
    def _():
        each(HALF, CELL, lambda step: query_copy(near_device(step)).start())
        send_near_context()

    mine[2].wait()
    mine[3].wait()
    start(*context_forwards(me))

    mine[1].wait()
    each(0, cell * KVH, lambda other: pass_on(other))
    each(0, cell * KVH, arrive_context)
    each(0, HALF, context_earlier)

    def relay_store(step):
        o = (head + step) % KVH * 2 + core
        for copy in store_forwards(o):
            copy.wait_recv()
        start(*store_forwards(o))

    each(1, KVH, relay_store)

    def arrive_store(other):
        for copy in store_forwards(other * 2 + 1 - core):
            copy.wait_recv()

    each(0, KVH, arrive_store)
    mine[0].wait()
    each(1, size, lambda step: table_arrival(step).wait_recv())

    lane = lax.broadcasted_iota(jnp.int32, (rows, HD), 1)

    def memory_states(b):
        q = [head_of(b, n) for n in range(PAIR)]
        steps = []
        for t in range(PICKS // PER_TILE):
            ks, vs, gone = [], [], []
            for x in range(PER_TILE):
                pick = t * PER_TILE + x
                there = tb[b, pick % CAP * (HD // CAP) + cell * CELL + pick // CAP]
                at = pick // CAP * local + jnp.maximum(there, 0)
                ks.append(sk[at])
                vs.append(sv[at])
                gone.append(jnp.where(there < 0, NEG, 0.0).astype(jnp.float32))
            k, v = jnp.concatenate(ks, axis=0), jnp.concatenate(vs, axis=0)

            def hide(s, gone=gone):
                return jnp.concatenate(
                    [s[:, x * MROWS:(x + 1) * MROWS] + gone[x] for x in range(PER_TILE)], axis=1
                )

            steps += [(n, q[n], k, v, hide if masked else None) for n in range(PAIR)]
        return run_steps((None, None), steps)

    def serve_half(c, part):
        away = (cell + 1 + c) % cells
        first = ((cell - away + cells - 1) // cells + part) % 2 * HALF

        def serve(k, stats):
            b = away * CELL + first + k
            query_arrival(b).wait_recv()
            states = memory_states(b)
            slot = c * CELL + first + k
            for n in range(PAIR):
                m, l, acc = states[n]
                po[slot, :, n * HD:(n + 1) * HD] = (acc / l).astype(jnp.bfloat16)
                stats = jnp.where(lane == k * PAIR + n, m, stats)
                stats = jnp.where(lane == k * PAIR + n + STATS // 2, l, stats)
            partial_copy(slot).start()
            return stats

        stats = lax.fori_loop(0, HALF, serve, jnp.zeros((rows, HD), jnp.float32))
        ps[c * 2 + part] = stats.T[:STATS]
        stats_copy(c * 2 + part).start()

    def remember(step):
        b = near_device(step)
        i = b - cell * CELL

        for n, (m, l, acc) in enumerate(memory_states(b)):
            om[i, n] = m
            ol[i, n] = l
            oa[i, n] = acc

    for c in range(cells - 1):
        serve_half(c, 0)
    @pl.when(jnp.logical_not(close))
    def _():
        each(HALF, CELL, lambda step: query_copy(near_device(step)).start())
        send_near_context()

    for c in range(cells - 1):
        serve_half(c, 1)
    each(0, HALF, remember)
    each(HALF, CELL, context_earlier)
    each(HALF, CELL, remember)

    each(1, KVH, lambda step: pass_on(cell * KVH + (head + step) % KVH))
    each(cell * KVH, (cell + 1) * KVH, arrive_context)

    def finish(k, part):
        i = (inner + part) % 2 * HALF + k
        near = context_query(i)
        for c in range(cells - 1):
            partial_copy(c * CELL + i).wait_recv()
        for n in range(PAIR):
            m, l, acc = om[i, n], ol[i, n], oa[i, n]
            for c in range(cells - 1):
                there = rt[c * 2 + part]
                m_far = jnp.sum(jnp.where(lane == k * PAIR + n, there, 0.0), axis=-1, keepdims=True)
                l_far = jnp.sum(jnp.where(lane == k * PAIR + n + STATS // 2, there, 0.0), axis=-1, keepdims=True)
                top = jnp.maximum(m, m_far)
                w = jnp.exp2((m - top) * SCALE2)
                w_far = jnp.exp2((m_far - top) * SCALE2) * l_far
                far = ro[c * CELL + i, :, n * HD:(n + 1) * HD].astype(jnp.float32)
                m, l, acc = top, l * w + w_far, acc * w + far * w_far
            memory = (acc / l).astype(jnp.bfloat16).astype(jnp.float32)
            context = (near[n][2] / near[n][1]).astype(jnp.bfloat16).astype(jnp.float32)
            gate = 1.0 / (1.0 + jnp.exp(-jnp.full((1, HD), gate_ref[spot * PAIR + n], jnp.float32)))
            os[i, :, n * HD:(n + 1) * HD] = (gate * memory + (1.0 - gate) * context).astype(jnp.bfloat16)

        @pl.when(i == spot)
        def _():
            result_self().start()

        @pl.when(i != spot)
        def _():
            result_copy(i).start()

    for part in range(2):
        for c in range(cells - 1):
            x = c * 2 + part
            stats_copy(x).wait_recv()
            rt[x] = jnp.concatenate([rs[x], jnp.zeros((HD - STATS, rows), jnp.float32)], axis=0).T
        each(0, HALF, lambda k, part=part: finish(k, part))

    result_self().wait()
    each(1, CELL, lambda step: result_arrival((spot + step) % CELL).wait_recv())
    each(1, CELL, lambda step: result_copy((spot + step) % CELL).wait_send())
    each(1, size, lambda step: table_copy(step).wait_send())
    each(1, size, lambda step: query_copy((me + step) % size).wait_send())

    def drain_context(step):
        other = (chip + step) % chips

        @pl.when(other // KVH >= cell)
        def _():
            for copy in context_copies(other):
                copy.wait_send()

    each(1, chips, drain_context)

    def drain_forward(other):
        for copy in context_forwards(other * 2 + core):
            copy.wait_send()

    each(0, (cell + 1) * KVH, drain_forward)

    def drain_store_forward(other):
        for copy in store_forwards(other * 2 + core):
            copy.wait_send()

    each(0, KVH, drain_store_forward)
    each(0, (cells - 1) * CELL, lambda slot: partial_copy(slot).wait_send())
    each(0, 2 * (cells - 1), lambda x: stats_copy(x).wait_send())


def attention_call(gate, table, queries, keys, values, store_keys, store_values, size):
    rows = queries.shape[0]
    cells = size // CELL
    chips = size // 2
    local = store_keys.shape[0]
    far = max(cells - 1, 1)
    block = (rows, WIDTH)
    dma = pltpu.SemaphoreType.DMA
    return pl.pallas_call(
        functools.partial(attention_kernel, size, size * CAP != TOPM),
        out_shape=jax.ShapeDtypeStruct(queries.shape, jnp.bfloat16),
        in_specs=[pl.BlockSpec(memory_space=pltpu.SMEM)] + [pl.BlockSpec(memory_space=pl.ANY)] * 6,
        out_specs=pl.BlockSpec(memory_space=pltpu.VMEM),
        scratch_shapes=[
            pltpu.SMEM((size, HD), jnp.int32),
            pltpu.VMEM((size, *block), jnp.bfloat16),
            pltpu.VMEM((size, rows, HD), jnp.bfloat16),
            pltpu.VMEM((size, rows, HD), jnp.bfloat16),
            pltpu.VMEM((CELL * local, MROWS, HD), jnp.bfloat16),
            pltpu.VMEM((CELL * local, MROWS, HD), jnp.bfloat16),
            pltpu.VMEM((CELL, PAIR, rows, 1), jnp.float32),
            pltpu.VMEM((CELL, PAIR, rows, 1), jnp.float32),
            pltpu.VMEM((CELL, PAIR, rows, HD), jnp.float32),
            pltpu.VMEM((CELL, PAIR, rows, 1), jnp.float32),
            pltpu.VMEM((CELL, PAIR, rows, 1), jnp.float32),
            pltpu.VMEM((CELL, PAIR, rows, HD), jnp.float32),
            pltpu.VMEM((far * CELL, *block), jnp.bfloat16),
            pltpu.VMEM((far * CELL, *block), jnp.bfloat16),
            pltpu.VMEM((2 * far, STATS, rows), jnp.float32),
            pltpu.VMEM((2 * far, STATS, rows), jnp.float32),
            pltpu.VMEM((2 * far, rows, HD), jnp.float32),
            pltpu.VMEM((CELL, *block), jnp.bfloat16),
            dma((2, size)),
            dma((2, size)),
            dma((2, chips)),
            dma((2, size)),
            dma((2, chips)),
            dma((2, KVH)),
            dma((2, CELL)),
            dma((2, KVH)),
            dma((2, far * CELL)),
            dma((2, 2 * far)),
            dma((2, CELL)),
            dma((7,)),
        ],
        compiler_params=pltpu.CompilerParams(
            collective_id=0, has_side_effects=True, vmem_limit_bytes=VMEM_LIMIT
        ),
        cost_estimate=pl.CostEstimate(
            flops=16 * 4096 * 256 * 512, bytes_accessed=20_000_000, transcendentals=16 * 4096 * 256
        ),
    )(gate, table, queries, keys, values, store_keys, store_values)


def on_device(
    queries, ctx_keys, ctx_values, store_keys, store_values, block_ids, block_slot, gate_logit
):
    size = lax.axis_size("seq")
    local_count = store_keys.shape[0]
    my_slots = lookup_slots(block_ids.reshape(-1), block_slot)
    table = request_table(my_slots, HD // CAP, local_count)
    return attention_call(gate_logit, table, queries, ctx_keys, ctx_values, store_keys, store_values, size)


def solution(mesh):
    placed = (
        P(("groups", "seq"), None),
        P(("groups", "seq"), None),
        P(("groups", "seq"), None),
        P(("groups", "seq"), None, None),
        P(("groups", "seq"), None, None),
        P(("groups", "seq"), None),
        P("groups"),
        P(),
    )
    return jax.shard_map(
        on_device, mesh=mesh, in_specs=placed, out_specs=P(("groups", "seq"), None), check_vma=False
    )
```
